256 devices in a mesh: slab: 16 (over z_hi, x, core), chan: 16 (over y, z_lo).
Axes of the slice: x: 4, y: 4, z: 8 (z_hi: 2, z_lo: 4; z = z_hi * 4 + z_lo), core: 2. Of those that a mesh axis runs over, the one named last changes fastest.
Arguments:
- activations: bfloat16 [2, 128, 32, 16384], P(None, 'chan', 'slab'), may hold values from -6 to 6
- out_grad: bfloat16 [2, 256, 16, 4096], P(None, 'chan', 'slab'), may hold values from -6 to 6
- weights: bfloat16 [27, 128, 256], P(None, 'chan'), may hold values from -0.109375 to 0.109375
Outputs:
- input_grad: bfloat16 [2, 128, 32, 16384], P(None, 'chan', 'slab')
- weight_grad: float32 [27, 128, 256], P(None, 'chan', 'slab')
The draws below stay inside these ranges and needn't reach their ends.
All inputs are finite; a program needn't handle non-finite values.
Results may differ from the reference program's by a relative error of at most 0.001.
Values may be sent and summed in bfloat16 or wider, within the bound.
A program may use at most 128 MiB of HBM per device.

```python
import math
import jax
import jax.numpy as jnp
from jax import lax

CIN = 128
COUT = 256
EDGE = 128
SAMPLES = 2
DEPTH = 32


def strengthened(result, stream_key, source, target, shards_of, factor):
    def block_of(position):
        return (jnp.arange(result.shape[position]) // (result.shape[position] // shards_of)).reshape((-1,) + (1,) * (result.ndim - 1 - position))

    one_side = jax.random.permutation(stream_key, shards_of)[block_of(target)]
    second = (block_of(target) + shards_of // 2) % shards_of
    return jnp.where((block_of(source) == one_side) | (block_of(source) == second), factor * result, result)


def block_scale(own_key, shape, cuts, least, high):
    def one(axis_at, blocks):
        draws = jax.random.uniform(jax.random.fold_in(jax.random.fold_in(own_key, 6), axis_at), (blocks,), jnp.float32, least / len(cuts), high / len(cuts))
        return jnp.repeat(jnp.exp(draws), shape[axis_at] // blocks).reshape((-1,) + (1,) * (len(shape) - axis_at - 1))

    factor_of = one(*cuts[0])
    for cut in cuts[1:]:
        factor_of = factor_of * one(*cut)
    return factor_of


def centred(key, shape, spread, bound, split=(), kind=jnp.bfloat16):
    array = spread * jax.random.normal(key, shape, jnp.float32)
    if split:
        array = array * block_scale(key, shape, split, -0.22, 0.18)
    return jnp.clip(array, -bound, bound).astype(kind)


def heavy_noise(stream_key, dims, scale, most, cuts, heavy, held_as=jnp.bfloat16):
    array = scale * jax.random.normal(stream_key, dims, jnp.float32)
    if cuts:
        array = array * block_scale(stream_key, dims, cuts, -0.22, 0.18)
    return jnp.clip(strengthened(array, jax.random.fold_in(stream_key, 3), *heavy), -most, most).astype(held_as)


def setup_inputs(seed: int = 0) -> dict:
    seeds = jax.random.split(jax.random.key(seed), 4)
    return {
        "activations": centred(seeds[0], (SAMPLES, CIN, DEPTH, EDGE * EDGE), 1.0, 6.0, ((1, 16), (2, 16))),
        "out_grad": heavy_noise(seeds[1], (SAMPLES, COUT, DEPTH // 2, (EDGE // 2) * (EDGE // 2)), 1.0, 6.0, ((1, 16), (2, 16)), (2, 1, 16, 2.0)),
        "weights": centred(seeds[2], (27, CIN, COUT), (27 * CIN) ** -0.5, 0.109375, ((1, 16),)),
    }


def shift_back(values, which_axis):
    extent = list(values.shape)
    extent[which_axis] = 1
    zero_slab = jnp.zeros(tuple(extent), values.dtype)
    retained = lax.slice_in_dim(values, 0, values.shape[which_axis] - 1, axis=which_axis)
    return jnp.concatenate([zero_slab, retained], axis=which_axis)

def shift_ahead(values, which_axis):
    extent = list(values.shape)
    extent[which_axis] = 1
    zero_slab = jnp.zeros(tuple(extent), values.dtype)
    retained = lax.slice_in_dim(values, 1, values.shape[which_axis], axis=which_axis)
    return jnp.concatenate([retained, zero_slab], axis=which_axis)

def flat_back(values, amount):
    zero_part = jnp.zeros(values.shape[:-1] + (amount,), values.dtype)
    return jnp.concatenate([zero_part, values[..., :values.shape[-1] - amount]], axis=-1)

def flat_ahead(values, amount):
    zero_part = jnp.zeros(values.shape[:-1] + (amount,), values.dtype)
    return jnp.concatenate([values[..., amount:], zero_part], axis=-1)

def column_index(length, half_edge):
    return lax.iota(jnp.int32, length) % half_edge

def tap_view(volume, row_tap, col_tap, half_edge):
    cells = half_edge * half_edge
    row_phase = 0 if row_tap == 1 else 1
    col_phase = 0 if col_tap == 1 else 1
    block = row_phase * 2 + col_phase
    picked = volume[..., block * cells:(block + 1) * cells]
    if row_tap == 0:
        picked = flat_back(picked, half_edge)
    if col_tap == 0:
        picked = flat_back(picked, 1)
        keep_mask = column_index(cells, half_edge) != 0
        picked = jnp.where(keep_mask, picked, jnp.zeros_like(picked))
    return picked

def assemble(fetch, half_edge, block_cells, keep):
    last_column = column_index(block_cells, half_edge) == half_edge - 1

    def col_ahead(values):
        moved = flat_ahead(values, 1)
        return jnp.where(last_column, jnp.zeros_like(moved), moved)
    rows_even = [fetch(1, col_tap) for col_tap in range(3)]
    rows_odd = [fetch(2, col_tap) + flat_ahead(fetch(0, col_tap), half_edge) for col_tap in range(3)]
    phases = []
    for rows in (rows_even, rows_odd):
        phases.append(rows[1][..., :keep])
        phases.append((rows[2] + col_ahead(rows[0]))[..., :keep])
    return jnp.concatenate(phases, axis=-1)

def reference(activations, out_grad, weights):
    half_edge = EDGE // 2
    cells = half_edge * half_edge
    phased = activations.astype(jnp.float32).reshape(SAMPLES, CIN, DEPTH // 2, 2, EDGE * EDGE)
    even_planes = phased[:, :, :, 0]
    odd_planes = phased[:, :, :, 1]
    depth_views = (shift_back(odd_planes, 2), even_planes, odd_planes)
    signal = out_grad.astype(jnp.float32)
    signal_next = shift_ahead(signal, 2)
    grad_scale = 1.0 / math.sqrt(SAMPLES * (DEPTH // 2) * half_edge * half_edge)
    pieces = []
    for depth_tap in range(3):
        for row_tap in range(3):
            for col_tap in range(3):
                view = tap_view(depth_views[depth_tap], row_tap, col_tap, half_edge)
                pieces.append(jnp.einsum('bcdp,bkdp->ck', view, signal))
    weight_grad = jnp.stack(pieces) * grad_scale
    weights_wide = weights.astype(jnp.float32)
    folded = []
    for depth_tap in range(3):
        source = signal_next if depth_tap == 0 else signal

        def fetch(row_tap, col_tap, depth_tap=depth_tap, source=source):
            return jnp.einsum('ck,bkdp->bcdp', weights_wide[9 * depth_tap + 3 * row_tap + col_tap], source)
        folded.append(assemble(fetch, half_edge, cells, cells))
    odd_out = folded[2] + folded[0]
    input_grad = jnp.stack([folded[1], odd_out], axis=3).reshape(SAMPLES, CIN, DEPTH, EDGE * EDGE).astype(jnp.bfloat16)
    return (input_grad, weight_grad)
```

```python
import functools
import math

import jax
import jax.numpy as jnp
from jax import lax
from jax.experimental import pallas as pl
from jax.experimental.pallas import tpu as pltpu
from jax.sharding import PartitionSpec as P

MESH = pl.DeviceIdType.MESH
EDGE = 128
HALF = EDGE // 2
CELLS = HALF * HALF
CHUNK = 1024
PER_SAMPLE = CELLS // CHUNK
CHUNKS = 2 * PER_SAMPLE
EARLY = tuple(range(9, 25))
LATE = (25, 26) + tuple(range(9))


def gather_kernel(
    grad_hbm, planes_hbm, w_ref, out_ref, wg_ref,
    held, early, late, planes, groups, carry, share, share_in,
    even, odd, acc, near, mine, far, far_in,
    local_sem, z_send, z_recv, y_send, y_recv, f_send, f_recv,
    halo_send, halo_recv, p_send, p_recv, r_send, r_recv, m_send, m_recv,
):
    slab = lax.axis_index("slab")
    chan = lax.axis_index("chan")
    y, z = chan // 4, chan % 4
    half, spot = slab // 8, slab % 8

    def at(slab_to, chan_to):
        return (slab_to, chan_to)

    along_z = [at(slab, y * 4 + (z + d) % 4) for d in range(1, 4)]
    y_up = at(slab, ((y + 1) % 4) * 4 + z)
    y_down = at(slab, ((y + 3) % 4) * 4 + z)
    near_to = [at(half * 8 + (spot + d) % 8, chan) for d in range(1, 8)]
    mirror = at((1 - half) * 8 + spot, chan)
    before = at(lax.max(slab - 1, 0), chan)
    after = at(lax.min(slab + 1, 15), chan)
    is_edge = (slab == 7) | (slab == 8)
    across = at(15 - slab, chan)

    barrier = pltpu.get_barrier_semaphore()
    peers = along_z + [y_up, y_down] + near_to + [mirror]
    for peer in peers:
        pl.semaphore_signal(barrier, inc=1, device_id=peer, device_id_type=MESH)

    @pl.when(is_edge)
    def _():
        pl.semaphore_signal(barrier, inc=1, device_id=across, device_id_type=MESH)

    own_rows = pl.ds(pl.multiple_of(chan * 16, 16), 16)

    def source(k):
        begin = pl.multiple_of((PER_SAMPLE - 1 - k % PER_SAMPLE) * CHUNK, CHUNK)
        return grad_hbm.at[k // PER_SAMPLE, :, pl.ds(begin, CHUNK)]

    def local(k):
        return pltpu.make_async_copy(source(k), held.at[k, own_rows], local_sem.at[k])

    def remote(src, dst, send, recv, to):
        return pltpu.make_async_remote_copy(
            src_ref=src, dst_ref=dst, send_sem=send, recv_sem=recv, device_id=to, device_id_type=MESH
        )

    def z_copies(k):
        return [
            remote(source(k), held.at[k, own_rows], z_send.at[k, d], z_recv.at[k, d], along_z[d])
            for d in range(3)
        ]

    block = pl.ds(pl.multiple_of(y * 64, 64), 64)
    up_block = pl.ds(pl.multiple_of(((y + 3) % 4) * 64, 64), 32)
    down_block = pl.ds(pl.multiple_of(((y + 1) % 4) * 64 + 32, 32), 32)

    def y_copies(k):
        return [
            remote(held.at[k, block], held.at[k, block], y_send.at[k, 0], y_recv.at[k, 0], y_up),
            remote(held.at[k, block], held.at[k, block], y_send.at[k, 1], y_recv.at[k, 1], y_down),
        ]

    def f_copies(k):
        return [
            remote(held.at[k, up_block], held.at[k, up_block], f_send.at[k, 0], f_recv.at[k, 0], y_up),
            remote(held.at[k, down_block], held.at[k, down_block], f_send.at[k, 1], f_recv.at[k, 1], y_down),
        ]

    halo = remote(planes_hbm.at[1], planes.at[0], halo_send, halo_recv, after)
    load_even = pltpu.make_async_copy(planes_hbm.at[0], planes.at[1], local_sem.at[CHUNKS])
    load_odd = pltpu.make_async_copy(planes_hbm.at[1], planes.at[2], local_sem.at[CHUNKS + 1])

    def share_copy(k):
        return remote(share.at[k], share_in.at[k], p_send.at[k], p_recv.at[k], before)

    load_even.start()
    load_odd.start()
    for k in range(CHUNKS):
        local(k).start()

    @pl.when(is_edge)
    def _():
        pl.semaphore_wait(barrier, len(peers) + 1)

    @pl.when(jnp.logical_not(is_edge))
    def _():
        pl.semaphore_wait(barrier, len(peers))

    for k in range(2):
        for copy in z_copies(k):
            copy.start()

    @pl.when(slab < 15)
    def _():
        halo.start()

    acc[...] = jnp.zeros_like(acc)
    far[...] = jnp.zeros_like(far)
    load_even.wait()
    load_odd.wait()

    lane = lax.broadcasted_iota(jnp.int32, (8, CELLS), 1)
    first_col = lane % HALF == 0
    first_row = lane < HALF

    def view(depth_tap, sample, row_tap, col_tap):
        at_block = (2 * (row_tap != 1) + (col_tap != 1)) * CELLS
        v = planes[depth_tap, sample, :, at_block : at_block + CELLS].astype(jnp.float32)
        amount = (HALF if row_tap == 0 else 0) + (1 if col_tap == 0 else 0)
        if amount:
            v = pltpu.roll(v, amount, 1)
            drop = first_col if col_tap == 0 else first_row
            if col_tap == 0 and row_tap == 0:
                drop = first_col | first_row
            v = jnp.where(drop, 0.0, v)
        return v

    def fill(store, taps):
        for sample in range(2):
            for pair in range((len(taps) + 1) // 2):
                rows = []
                for t in taps[2 * pair : 2 * pair + 2]:
                    rows.append(view(t // 9, sample, (t // 3) % 3, t % 3))
                if len(rows) == 1:
                    rows.append(jnp.zeros_like(rows[0]))
                both = jnp.concatenate(rows, axis=0).astype(jnp.bfloat16)
                for j in range(PER_SAMPLE):
                    store[sample * PER_SAMPLE + PER_SAMPLE - 1 - j, 16 * pair : 16 * pair + 16, :] = both[
                        :, j * CHUNK : (j + 1) * CHUNK
                    ]

    def start_y(k):
        local(k).wait()
        for copy in z_copies(k):
            copy.wait_recv()
        for copy in y_copies(k):
            copy.start()

    def start_f(k):
        for copy in y_copies(k):
            copy.wait_recv()
        for copy in f_copies(k):
            copy.start()

    start_y(0)
    fill(early, EARLY)

    chunk_lane = lax.broadcasted_iota(jnp.int32, (8, CHUNK), 1)
    last_col = chunk_lane % HALF == HALF - 1

    def row_ahead(value, tail):
        wide = jnp.concatenate([value, tail], axis=1)
        return pltpu.roll(wide, CHUNK + 128 - HALF, 1)[:, :CHUNK]

    def col_ahead(value):
        return jnp.where(last_col, 0.0, pltpu.roll(value, CHUNK - 1, 1))

    def phases(depth_tap):
        def fetch(row_tap, col_tap):
            row = 8 * (9 * depth_tap + 3 * row_tap + col_tap)
            return groups[row : row + 8, :]

        def odd_row(col_tap):
            at_carry = 3 * depth_tap + col_tap
            moving = fetch(0, col_tap)
            moved = row_ahead(moving, carry[at_carry])
            carry[at_carry] = moving[:, :128]
            return fetch(2, col_tap) + moved

        found = []
        rows_even = [fetch(1, c) for c in range(3)]
        rows_odd = [odd_row(c) for c in range(3)]
        for rows in (rows_even, rows_odd):
            found.append(rows[1])
            found.append(rows[2] + col_ahead(rows[0]))
        return found

    def lanes_of(k, phase):
        begin = phase * CELLS + (PER_SAMPLE - 1 - k % PER_SAMPLE) * CHUNK
        return pl.ds(pl.multiple_of(begin, CHUNK), CHUNK)

    def late_dot(k):
        term = lax.dot_general(
            held[k], late[k], (((1,), (1,)), ((), ())), preferred_element_type=jnp.float32
        )
        acc[:, :, :, 128:224] += term.reshape(2, 8, 16, 96)

    def finish(k):
        @pl.when(slab < 15)
        def _():
            share_copy(k).wait_recv()

        for phase in range(4):
            value = odd[k % 2, phase]
            inward = jnp.where(slab < 15, share_in[k, phase], 0.0)
            out_ref[1, k // PER_SAMPLE, :, lanes_of(k, phase)] = (value + inward).astype(jnp.bfloat16)

    def step(i, _):
        k = i

        @pl.when(i + 3 < CHUNKS)
        def _():
            for copy in z_copies(i + 3):
                copy.start()

        @pl.when(i + 2 < CHUNKS)
        def _():
            start_y(i + 2)

        @pl.when(i + 1 < CHUNKS)
        def _():
            start_f(i + 1)

        for copy in f_copies(k):
            copy.wait_recv()

        @pl.when(k % PER_SAMPLE == 0)
        def _():
            carry[...] = jnp.zeros_like(carry)

        groups[...] = jnp.dot(w_ref[...], held[k], preferred_element_type=jnp.float32)
        for phase, value in enumerate(phases(0)):
            share[k, phase] = value

        @pl.when(slab > 0)
        def _():
            share_copy(k).start()

        for phase, value in enumerate(phases(1)):
            out_ref[0, k // PER_SAMPLE, :, lanes_of(k, phase)] = value.astype(jnp.bfloat16)
        for phase, value in enumerate(phases(2)):
            odd[k % 2, phase] = value

        term = lax.dot_general(
            held[k], early[k], (((1,), (1,)), ((), ())), preferred_element_type=jnp.float32
        )
        acc[:, :, :, :128] += term.reshape(2, 8, 16, 128)

        @pl.when(k == CHUNKS - 2)
        def _():
            @pl.when(slab > 0)
            def _():
                halo.wait_recv()

            @pl.when(slab == 0)
            def _():
                planes[0] = jnp.zeros_like(planes[0])

            fill(late, LATE)

            def catch_up(n, _):
                late_dot(n)
                return 0

            lax.fori_loop(0, CHUNKS - 2, catch_up, 0)

        @pl.when(k >= CHUNKS - 2)
        def _():
            late_dot(k)

        @pl.when(k >= 1)
        def _():
            finish(k - 1)

        return 0

    for copy in z_copies(2):
        copy.start()
    start_y(1)
    start_f(0)
    lax.fori_loop(0, CHUNKS, step, 0)

    def near_copy(d):
        return remote(acc.at[:, (spot + d + 1) % 8], near.at[d], r_send.at[d], r_recv.at[d], near_to[d])

    for d in range(7):
        near_copy(d).start()
    finish(CHUNKS - 1)
    for d in range(7):
        near_copy(d).wait_recv()
    total = acc[:, spot]
    for d in range(7):
        total = total + near[d]
    mine[...] = total
    far[...] = mine[1 - half]
    last = remote(far, far_in, m_send, m_recv, mirror)
    last.start()
    last.wait_recv()
    scale = 1.0 / math.sqrt(2 * 16 * CELLS)
    wg_ref[...] = (mine[half] + far_in[...]) * scale

    last.wait_send()
    for d in range(7):
        near_copy(d).wait_send()

    def drain(k, _):
        for copy in z_copies(k) + y_copies(k) + f_copies(k):
            copy.wait_send()

        @pl.when(slab > 0)
        def _():
            share_copy(k).wait_send()

        return 0

    lax.fori_loop(0, CHUNKS, drain, 0)

    @pl.when(slab < 15)
    def _():
        halo.wait_send()


def body(activations, out_grad, weights):
    planes = activations.transpose(2, 0, 1, 3)
    grad = out_grad.reshape(2, 16, CELLS)
    w = weights.reshape(216, 256)
    sem = pltpu.SemaphoreType.DMA
    f32, bf16 = jnp.float32, jnp.bfloat16
    any_space = pl.BlockSpec(memory_space=pl.ANY)
    vmem = pl.BlockSpec(memory_space=pltpu.VMEM)
    out, wg = pl.pallas_call(
        gather_kernel,
        out_shape=(
            jax.ShapeDtypeStruct((2, 2, 8, 4 * CELLS), bf16),
            jax.ShapeDtypeStruct((16, 256), f32),
        ),
        in_specs=[any_space, any_space, vmem],
        out_specs=(vmem, vmem),
        scratch_shapes=[
            pltpu.VMEM((CHUNKS, 256, CHUNK), bf16),
            pltpu.VMEM((CHUNKS, 128, CHUNK), bf16),
            pltpu.VMEM((CHUNKS, 96, CHUNK), bf16),
            pltpu.VMEM((3, 2, 8, 4 * CELLS), bf16),
            pltpu.VMEM((216, CHUNK), f32),
            pltpu.VMEM((9, 8, 128), f32),
            pltpu.VMEM((CHUNKS, 4, 8, CHUNK), f32),
            pltpu.VMEM((CHUNKS, 4, 8, CHUNK), f32),
            pltpu.VMEM((1, 8, 128), f32),
            pltpu.VMEM((2, 4, 8, CHUNK), f32),
            pltpu.VMEM((2, 8, 16, 256), f32),
            pltpu.VMEM((7, 2, 16, 256), f32),
            pltpu.VMEM((2, 16, 256), f32),
            pltpu.VMEM((16, 256), f32),
            pltpu.VMEM((16, 256), f32),
            sem((CHUNKS + 2,)),
            sem((CHUNKS, 3)), sem((CHUNKS, 3)),
            sem((CHUNKS, 2)), sem((CHUNKS, 2)),
            sem((CHUNKS, 2)), sem((CHUNKS, 2)),
            sem, sem,
            sem((CHUNKS,)), sem((CHUNKS,)),
            sem((7,)), sem((7,)),
            sem, sem,
        ],
        compiler_params=pltpu.CompilerParams(
            collective_id=0, has_side_effects=True, vmem_limit_bytes=48 * 1024 * 1024
        ),
    )(grad, planes, w)
    input_grad = out.transpose(1, 2, 0, 3)
    taps = wg[:, :216].reshape(16, 27, 8)
    taps = jnp.concatenate([taps[:, 18:], taps[:, :18]], axis=1)
    return input_grad, taps.transpose(1, 2, 0)


def solution(mesh):
    placed = (P(None, "chan", "slab", None), P(None, "chan", "slab", None), P(None, "chan", None))
    return jax.shard_map(
        body,
        mesh=mesh,
        in_specs=placed,
        out_specs=(P(None, "chan", "slab", None), P(None, "chan", "slab")),
        check_vma=False,
    )
```

```python
import functools
import math

import jax
import jax.numpy as jnp
from jax import lax
from jax.experimental import pallas as pl
from jax.experimental.pallas import tpu as pltpu
from jax.sharding import PartitionSpec as P

MESH = pl.DeviceIdType.MESH
EDGE = 128
HALF = EDGE // 2
CELLS = HALF * HALF
CHUNK = 1024
PER_SAMPLE = CELLS // CHUNK
CHUNKS = 2 * PER_SAMPLE
EARLY = tuple(range(9, 25))
HALO_AT = 4
LATE = (25, 26) + tuple(range(9))


def gather_kernel(
    grad_hbm, planes_hbm, w_ref, out_ref, wg_ref,
    held, early, late, planes, groups, carry, share, share_in,
    odd, acc, pair_in, paired, near, mine, far, far_in, relay, halo_relay,
    local_sem, z_send, z_recv, y_send, y_recv, f_send, f_recv,
    halo_send, halo_recv, p_send, p_recv, q_send, q_recv, h_send, h_recv,
    c_send, c_recv, r_send, r_recv, m_send, m_recv,
):
    slab = lax.axis_index("slab")
    chan = lax.axis_index("chan")
    y, z = chan // 4, chan % 4
    half, spot = slab // 8, slab % 8

    def at(slab_to, chan_to):
        return (slab_to, chan_to)

    along_z = [at(slab, y * 4 + (z + d) % 4) for d in range(1, 4)]
    y_up = at(slab, ((y + 1) % 4) * 4 + z)
    y_down = at(slab, ((y + 3) % 4) * 4 + z)
    column, core = spot // 2, spot % 2
    near_to = [at(half * 8 + (spot + d) % 8, chan) for d in range(1, 8)]
    pair = at(slab + 1 - 2 * core, chan)
    along_x = [at(half * 8 + (spot + 2 * d) % 8, chan) for d in range(1, 4)]
    mirror = at((1 - half) * 8 + spot, chan)
    before = at(lax.max(slab - 1, 0), chan)
    after = at(lax.min(slab + 1, 15), chan)
    low_side = (slab < 6) & (core == 1)
    high_side = (slab > 8) & (core == 0)

    barrier = pltpu.get_barrier_semaphore()
    peers = along_z + [y_up, y_down] + near_to + [mirror]

    def greet(peer):
        pl.semaphore_signal(barrier, inc=1, device_id=peer, device_id_type=MESH)

    for peer in peers:
        greet(peer)

    @pl.when(slab == 7)
    def _():
        for q in range(4):
            greet(at(8 + 2 * q, chan))

    @pl.when(slab == 8)
    def _():
        for q in range(4):
            greet(at(1 + 2 * q, chan))

    @pl.when(low_side)
    def _():
        greet(at(8, chan))

    @pl.when(high_side)
    def _():
        greet(at(7, chan))

    own_rows = pl.ds(pl.multiple_of(chan * 16, 16), 16)

    def source(k):
        begin = pl.multiple_of((PER_SAMPLE - 1 - k % PER_SAMPLE) * CHUNK, CHUNK)
        return grad_hbm.at[k // PER_SAMPLE, :, pl.ds(begin, CHUNK)]

    def local(k):
        return pltpu.make_async_copy(source(k), held.at[k, own_rows], local_sem.at[k])

    def remote(src, dst, send, recv, to):
        return pltpu.make_async_remote_copy(
            src_ref=src, dst_ref=dst, send_sem=send, recv_sem=recv, device_id=to, device_id_type=MESH
        )

    def z_copies(k):
        return [
            remote(source(k), held.at[k, own_rows], z_send.at[k, d], z_recv.at[k, d], along_z[d])
            for d in range(3)
        ]

    block = pl.ds(pl.multiple_of(y * 64, 64), 64)
    up_block = pl.ds(pl.multiple_of(((y + 3) % 4) * 64, 64), 32)
    down_block = pl.ds(pl.multiple_of(((y + 1) % 4) * 64 + 32, 32), 32)

    def y_copies(k):
        return [
            remote(held.at[k, block], held.at[k, block], y_send.at[k, 0], y_recv.at[k, 0], y_up),
            remote(held.at[k, block], held.at[k, block], y_send.at[k, 1], y_recv.at[k, 1], y_down),
        ]

    def f_copies(k):
        return [
            remote(held.at[k, up_block], held.at[k, up_block], f_send.at[k, 0], f_recv.at[k, 0], y_up),
            remote(held.at[k, down_block], held.at[k, down_block], f_send.at[k, 1], f_recv.at[k, 1], y_down),
        ]

    halo = remote(planes_hbm.at[1], planes.at[0], halo_send.at[0], halo_recv.at[0], after)

    def quarter(q):
        return pl.ds(pl.multiple_of(q * CELLS, CELLS), CELLS)

    def halo_out(q):
        if q == 3:
            return remote(
                planes_hbm.at[1, :, :, quarter(3)], planes.at[0, :, :, quarter(3)],
                halo_send.at[3], halo_recv.at[3], at(8, chan),
            )
        return remote(
            planes_hbm.at[1, :, :, quarter(q)], halo_relay,
            halo_send.at[q], h_recv, at(1 + 2 * q, chan),
        )

    halo_on = remote(
        halo_relay, planes.at[0, :, :, quarter(column)], h_send, halo_recv.at[column], at(8, chan)
    )
    load_even = pltpu.make_async_copy(planes_hbm.at[0], planes.at[1], local_sem.at[CHUNKS])
    load_odd = pltpu.make_async_copy(planes_hbm.at[1], planes.at[2], local_sem.at[CHUNKS + 1])

    def share_copy(k, q):
        return remote(share.at[k, q], share_in.at[k, q], p_send.at[k, q], p_recv.at[k, q], before)

    def share_out(k, q):
        if q == 0:
            return share_copy(k, 0)
        return remote(share.at[k, q], relay.at[k], p_send.at[k, q], q_recv.at[k], at(8 + 2 * q, chan))

    def share_on(k):
        return remote(relay.at[k], share_in.at[k, column], q_send.at[k], p_recv.at[k, column], at(7, chan))

    def send_share(k):
        @pl.when((slab > 0) & (slab != 8))
        def _():
            for q in range(4):
                share_copy(k, q).start()

        @pl.when(slab == 8)
        def _():
            for q in (1, 2, 3, 0):
                share_out(k, q).start()

    def pass_share(k):
        @pl.when(high_side)
        def _():
            share_out(k, 1).wait_recv()
            share_on(k).start()

    load_even.start()
    load_odd.start()
    for k in range(CHUNKS):
        local(k).start()

    is_edge = (slab == 7) | (slab == 8)
    is_side = low_side | high_side

    @pl.when(is_edge)
    def _():
        pl.semaphore_wait(barrier, len(peers) + 4)

    @pl.when(is_side)
    def _():
        pl.semaphore_wait(barrier, len(peers) + 1)

    @pl.when(jnp.logical_not(is_edge | is_side))
    def _():
        pl.semaphore_wait(barrier, len(peers))

    for k in range(CHUNKS):
        for copy in z_copies(k):
            copy.start()

    @pl.when((slab < 15) & (slab != 7))
    def _():
        halo.start()

    @pl.when(slab == 7)
    def _():
        for q in range(4):
            halo_out(q).start()

    acc[...] = jnp.zeros_like(acc)
    load_even.wait()
    load_odd.wait()

    lane = lax.broadcasted_iota(jnp.int32, (8, CELLS), 1)
    first_col = lane % HALF == 0
    first_row = lane < HALF

    def view(depth_tap, sample, row_tap, col_tap):
        at_block = (2 * (row_tap != 1) + (col_tap != 1)) * CELLS
        v = planes[depth_tap, sample, :, at_block : at_block + CELLS].astype(jnp.float32)
        amount = (HALF if row_tap == 0 else 0) + (1 if col_tap == 0 else 0)
        if amount:
            v = pltpu.roll(v, amount, 1)
            drop = first_col if col_tap == 0 else first_row
            if col_tap == 0 and row_tap == 0:
                drop = first_col | first_row
            v = jnp.where(drop, 0.0, v)
        return v

    def fill(store, taps):
        for sample in range(2):
            for pair in range((len(taps) + 1) // 2):
                rows = []
                for t in taps[2 * pair : 2 * pair + 2]:
                    rows.append(view(t // 9, sample, (t // 3) % 3, t % 3))
                if len(rows) == 1:
                    rows.append(jnp.zeros_like(rows[0]))
                both = jnp.concatenate(rows, axis=0).astype(jnp.bfloat16)
                for j in range(PER_SAMPLE):
                    store[sample * PER_SAMPLE + PER_SAMPLE - 1 - j, 16 * pair : 16 * pair + 16, :] = both[
                        :, j * CHUNK : (j + 1) * CHUNK
                    ]

    def start_y(k):
        local(k).wait()
        for copy in z_copies(k):
            copy.wait_recv()
        for copy in y_copies(k):
            copy.start()

    def start_f(k):
        for copy in y_copies(k):
            copy.wait_recv()
        for copy in f_copies(k):
            copy.start()

    start_y(0)
    fill(early, EARLY)

    chunk_lane = lax.broadcasted_iota(jnp.int32, (8, CHUNK), 1)
    last_col = chunk_lane % HALF == HALF - 1

    def row_ahead(value, tail):
        wide = jnp.concatenate([value, tail], axis=1)
        return pltpu.roll(wide, CHUNK + 128 - HALF, 1)[:, :CHUNK]

    def col_ahead(value):
        return jnp.where(last_col, 0.0, pltpu.roll(value, CHUNK - 1, 1))

    def phases(depth_tap):
        def fetch(row_tap, col_tap):
            row = 8 * (9 * depth_tap + 3 * row_tap + col_tap)
            return groups[row : row + 8, :]

        def odd_row(col_tap):
            at_carry = 3 * depth_tap + col_tap
            moving = fetch(0, col_tap)
            moved = row_ahead(moving, carry[at_carry])
            carry[at_carry] = moving[:, :128]
            return fetch(2, col_tap) + moved

        found = []
        rows_even = [fetch(1, c) for c in range(3)]
        rows_odd = [odd_row(c) for c in range(3)]
        for rows in (rows_even, rows_odd):
            found.append(rows[1])
            found.append(rows[2] + col_ahead(rows[0]))
        return found

    def lanes_of(k, phase):
        begin = phase * CELLS + (PER_SAMPLE - 1 - k % PER_SAMPLE) * CHUNK
        return pl.ds(pl.multiple_of(begin, CHUNK), CHUNK)

    def late_dot(k):
        term = lax.dot_general(
            held[k], late[k], (((1,), (1,)), ((), ())), preferred_element_type=jnp.float32
        )
        acc[:, :, :, :, 128:224] += term.reshape(2, 4, 2, 16, 96)

    def finish(k):
        @pl.when(slab < 15)
        def _():
            for q in range(4):
                share_copy(k, q).wait_recv()

        for phase in range(4):
            value = odd[k % 2, phase]
            inward = jnp.where(slab < 15, share_in[k, phase], 0.0)
            out_ref[1, k // PER_SAMPLE, :, lanes_of(k, phase)] = (value + inward).astype(jnp.bfloat16)

    def early_dot(k):
        term = lax.dot_general(
            held[k], early[k], (((1,), (1,)), ((), ())), preferred_element_type=jnp.float32
        )
        acc[:, :, :, :, :128] += term.reshape(2, 4, 2, 16, 128)

    def input_part(k):
        @pl.when(k % PER_SAMPLE == 0)
        def _():
            carry[...] = jnp.zeros_like(carry)

        groups[...] = jnp.dot(w_ref[...], held[k], preferred_element_type=jnp.float32)
        for phase, value in enumerate(phases(0)):
            share[k, phase] = value
        send_share(k)
        for phase, value in enumerate(phases(1)):
            out_ref[0, k // PER_SAMPLE, :, lanes_of(k, phase)] = value.astype(jnp.bfloat16)
        for phase, value in enumerate(phases(2)):
            odd[k % 2, phase] = value

    def receive(k):
        for copy in f_copies(k):
            copy.wait_recv()

    def step(k, _):
        @pl.when(k + 2 < CHUNKS)
        def _():
            start_y(k + 2)

        start_f(k + 1)
        receive(k)
        input_part(k)
        early_dot(k)

        @pl.when(k == HALO_AT)
        def _():
            @pl.when((slab > 0) & (slab != 8))
            def _():
                halo.wait_recv()

            @pl.when(slab == 8)
            def _():
                for q in range(4):
                    pltpu.make_async_remote_copy(
                        src_ref=planes.at[0, :, :, quarter(q)], dst_ref=planes.at[0, :, :, quarter(q)],
                        send_sem=h_send, recv_sem=halo_recv.at[q], device_id=mirror, device_id_type=MESH,
                    ).wait_recv()

            @pl.when(slab == 0)
            def _():
                planes[0] = jnp.zeros_like(planes[0])

            fill(late, LATE)

            def catch_up(n, _):
                late_dot(n)
                return 0

            lax.fori_loop(0, HALO_AT, catch_up, 0)

        @pl.when(k == 1)
        def _():
            @pl.when(low_side)
            def _():
                halo_out(0).wait_recv()
                halo_on.start()

        @pl.when(k >= HALO_AT)
        def _():
            late_dot(k)

        @pl.when(k >= 1)
        def _():
            pass_share(k - 1)
            finish(k - 1)

        return 0

    start_y(1)
    start_f(0)
    lax.fori_loop(0, CHUNKS - 1, step, 0)

    end = CHUNKS - 1
    pair_copy = remote(acc.at[:, :, 1 - core], pair_in, c_send, c_recv, pair)

    def near_copy(d):
        return remote(paired.at[:, (column + d + 1) % 4], near.at[d], r_send.at[d], r_recv.at[d], along_x[d])

    receive(end)
    early_dot(end)
    late_dot(end)
    pair_copy.start()
    input_part(end)
    pass_share(end - 1)
    pair_copy.wait_recv()
    paired[...] = acc[:, :, core] + pair_in[...]
    for d in range(3):
        near_copy(d).start()
    pass_share(end)
    finish(end - 1)
    for d in range(3):
        near_copy(d).wait_recv()
    mine[...] = paired[:, column] + near[0] + near[1] + near[2]
    far[...] = mine[1 - half]
    last = remote(far, far_in, m_send, m_recv, mirror)
    last.start()
    finish(end)
    last.wait_recv()
    scale = 1.0 / math.sqrt(2 * 16 * CELLS)
    wg_ref[...] = (mine[half] + far_in[...]) * scale

    last.wait_send()
    pair_copy.wait_send()
    for d in range(3):
        near_copy(d).wait_send()

    def drain(k, _):
        for copy in z_copies(k) + y_copies(k) + f_copies(k):
            copy.wait_send()

        @pl.when(slab > 0)
        def _():
            for q in range(4):
                share_copy(k, q).wait_send()

        @pl.when(high_side)
        def _():
            share_on(k).wait_send()

        return 0

    lax.fori_loop(0, CHUNKS, drain, 0)

    @pl.when((slab < 15) & (slab != 7))
    def _():
        halo.wait_send()

    @pl.when(slab == 7)
    def _():
        for q in range(4):
            halo_out(q).wait_send()

    @pl.when(low_side)
    def _():
        halo_on.wait_send()


def body(activations, out_grad, weights):
    planes = activations.transpose(2, 0, 1, 3)
    grad = out_grad.reshape(2, 16, CELLS)
    w = weights.reshape(216, 256)
    sem = pltpu.SemaphoreType.DMA
    f32, bf16 = jnp.float32, jnp.bfloat16
    any_space = pl.BlockSpec(memory_space=pl.ANY)
    vmem = pl.BlockSpec(memory_space=pltpu.VMEM)
    out, wg = pl.pallas_call(
        gather_kernel,
        out_shape=(
            jax.ShapeDtypeStruct((2, 2, 8, 4 * CELLS), bf16),
            jax.ShapeDtypeStruct((16, 256), f32),
        ),
        in_specs=[any_space, any_space, vmem],
        out_specs=(vmem, vmem),
        scratch_shapes=[
            pltpu.VMEM((CHUNKS, 256, CHUNK), bf16),
            pltpu.VMEM((CHUNKS, 128, CHUNK), bf16),
            pltpu.VMEM((CHUNKS, 96, CHUNK), bf16),
            pltpu.VMEM((3, 2, 8, 4 * CELLS), bf16),
            pltpu.VMEM((216, CHUNK), f32),
            pltpu.VMEM((9, 8, 128), f32),
            pltpu.VMEM((CHUNKS, 4, 8, CHUNK), f32),
            pltpu.VMEM((CHUNKS, 4, 8, CHUNK), f32),
            pltpu.VMEM((2, 4, 8, CHUNK), f32),
            pltpu.VMEM((2, 4, 2, 16, 256), f32),
            pltpu.VMEM((2, 4, 16, 256), f32),
            pltpu.VMEM((2, 4, 16, 256), f32),
            pltpu.VMEM((3, 2, 16, 256), f32),
            pltpu.VMEM((2, 16, 256), f32),
            pltpu.VMEM((16, 256), f32),
            pltpu.VMEM((16, 256), f32),
            pltpu.VMEM((CHUNKS, 8, CHUNK), f32),
            pltpu.VMEM((2, 8, CELLS), bf16),
            sem((CHUNKS + 2,)),
            sem((CHUNKS, 3)), sem((CHUNKS, 3)),
            sem((CHUNKS, 2)), sem((CHUNKS, 2)),
            sem((CHUNKS, 2)), sem((CHUNKS, 2)),
            sem((4,)), sem((4,)),
            sem((CHUNKS, 4)), sem((CHUNKS, 4)),
            sem((CHUNKS,)), sem((CHUNKS,)),
            sem, sem,
            sem, sem,
            sem((3,)), sem((3,)),
            sem, sem,
        ],
        compiler_params=pltpu.CompilerParams(
            collective_id=0, has_side_effects=True, vmem_limit_bytes=48 * 1024 * 1024
        ),
    )(grad, planes, w)
    input_grad = out.transpose(1, 2, 0, 3)
    taps = wg[:, :216].reshape(16, 27, 8)
    taps = jnp.concatenate([taps[:, 18:], taps[:, :18]], axis=1)
    return input_grad, taps.transpose(1, 2, 0)


def solution(mesh):
    placed = (P(None, "chan", "slab", None), P(None, "chan", "slab", None), P(None, "chan", None))
    return jax.shard_map(
        body,
        mesh=mesh,
        in_specs=placed,
        out_specs=(P(None, "chan", "slab", None), P(None, "chan", "slab")),
        check_vma=False,
    )
```

```python
import functools
import math

import jax
import jax.numpy as jnp
from jax import lax
from jax.experimental import pallas as pl
from jax.experimental.pallas import tpu as pltpu
from jax.sharding import PartitionSpec as P

MESH = pl.DeviceIdType.MESH
EDGE = 128
HALF = EDGE // 2
CELLS = HALF * HALF
CHUNK = 1024
PER_SAMPLE = CELLS // CHUNK
CHUNKS = 2 * PER_SAMPLE
EARLY = tuple(range(9, 25))
HALO_AT = 4
CROSS = CHUNKS - 1
LATE = (25, 26) + tuple(range(9))


def gather_kernel(
    grad_hbm, planes_hbm, w_ref, out_ref, wg_ref,
    held, early, late, planes, groups, carry, share, share_in,
    odd, acc, pair_in, paired, near, relay, halo_relay,
    local_sem, z_send, z_recv, y_send, y_recv, f_send, f_recv,
    halo_send, halo_recv, p_send, p_recv, q_send, q_recv, h_send, h_recv,
    c_send, c_recv, r_send, r_recv, by_send, by_recv, bf_send, bf_recv, bz_send, bz_recv,
):
    slab = lax.axis_index("slab")
    chan = lax.axis_index("chan")
    y, z = chan // 4, chan % 4
    half, spot = slab // 8, slab % 8

    def at(slab_to, chan_to):
        return (slab_to, chan_to)

    along_z = [at(slab, y * 4 + (z + d) % 4) for d in range(1, 4)]
    y_up = at(slab, ((y + 1) % 4) * 4 + z)
    y_down = at(slab, ((y + 3) % 4) * 4 + z)
    column, core = spot // 2, spot % 2
    near_to = [at(half * 8 + (spot + d) % 8, chan) for d in range(1, 8)]
    pair = at(slab + 1 - 2 * core, chan)
    place = half * 4 + column

    def core_peer(d):
        to = (place + d) % 8
        return at((to // 4) * 8 + (to % 4) * 2 + core, chan)

    spread_to = [core_peer(d) for d in range(1, 8)]
    across = [at((1 - half) * 8 + (spot + 2 * d) % 8, chan) for d in range(4)]
    mirror = at((1 - half) * 8 + spot, chan)
    before = at(lax.max(slab - 1, 0), chan)
    after = at(lax.min(slab + 1, 15), chan)
    low_side = (slab < 6) & (core == 1)
    high_side = (slab > 8) & (core == 0)

    barrier = pltpu.get_barrier_semaphore()
    peers = along_z + [y_up, y_down] + near_to + across

    def greet(peer):
        pl.semaphore_signal(barrier, inc=1, device_id=peer, device_id_type=MESH)

    for peer in peers:
        greet(peer)

    @pl.when(slab == 7)
    def _():
        for q in range(4):
            greet(at(8 + 2 * q, chan))

    @pl.when(slab == 8)
    def _():
        for q in range(4):
            greet(at(1 + 2 * q, chan))

    @pl.when(low_side)
    def _():
        greet(at(8, chan))

    @pl.when(high_side)
    def _():
        greet(at(7, chan))

    def source(k):
        begin = pl.multiple_of((PER_SAMPLE - 1 - k % PER_SAMPLE) * CHUNK, CHUNK)
        return grad_hbm.at[k // PER_SAMPLE, :, pl.ds(begin, CHUNK)]

    def local(k):
        return pltpu.make_async_copy(source(k), held.at[k, y, z], local_sem.at[k])

    def remote(src, dst, send, recv, to):
        return pltpu.make_async_remote_copy(
            src_ref=src, dst_ref=dst, send_sem=send, recv_sem=recv, device_id=to, device_id_type=MESH
        )

    def z_copies(k):
        return [
            remote(source(k), held.at[k, y, z], z_send.at[k, d], z_recv.at[k, d], along_z[d])
            for d in range(3)
        ]

    low, high = (y + 3) % 4, (y + 1) % 4

    def y_copies(k):
        block = held.at[k, y]
        return [
            remote(block, block, y_send.at[k, 0], y_recv.at[k, 0], y_up),
            remote(block, block, y_send.at[k, 1], y_recv.at[k, 1], y_down),
        ]

    def f_copies(k):
        from_low, from_high = held.at[k, low, pl.ds(0, 2)], held.at[k, high, pl.ds(2, 2)]
        return [
            remote(from_low, from_low, f_send.at[k, 0], f_recv.at[k, 0], y_up),
            remote(from_high, from_high, f_send.at[k, 1], f_recv.at[k, 1], y_down),
        ]

    def cross_y():
        return [
            remote(source(CROSS), held.at[CROSS, y, z], by_send.at[0], by_recv.at[0], y_up),
            remote(source(CROSS), held.at[CROSS, y, z], by_send.at[1], by_recv.at[1], y_down),
        ]

    def cross_f():
        from_low = held.at[CROSS, low, z, :, pl.ds(0, CHUNK // 2)]
        from_high = held.at[CROSS, high, z, :, pl.ds(CHUNK // 2, CHUNK // 2)]
        return [
            remote(from_low, from_low, bf_send.at[0], bf_recv.at[0], y_up),
            remote(from_high, from_high, bf_send.at[1], bf_recv.at[1], y_down),
        ]

    z_up = at(slab, y * 4 + lax.min(z + 1, 3))
    z_down = at(slab, y * 4 + lax.max(z - 1, 0))

    def cross_up(hop):
        piece = held.at[CROSS, :, lax.max(z - hop, 0)]
        return remote(piece, piece, bz_send.at[0, hop], bz_recv.at[0, hop], z_up)

    def cross_down(hop):
        piece = held.at[CROSS, :, lax.min(z + hop, 3)]
        return remote(piece, piece, bz_send.at[1, hop], bz_recv.at[1, hop], z_down)

    def cross_send(hop):
        @pl.when((z < 3) & (z >= hop))
        def _():
            cross_up(hop).start()

        @pl.when((z > 0) & (z + hop <= 3))
        def _():
            cross_down(hop).start()

    def cross_wait_send(hop):
        @pl.when((z < 3) & (z >= hop))
        def _():
            cross_up(hop).wait_send()

        @pl.when((z > 0) & (z + hop <= 3))
        def _():
            cross_down(hop).wait_send()

    def cross_recv(hop):
        @pl.when(z > hop)
        def _():
            cross_up(hop).wait_recv()

        @pl.when(z + hop < 3)
        def _():
            cross_down(hop).wait_recv()

    halo = remote(planes_hbm.at[1], planes.at[0], halo_send.at[0], halo_recv.at[0], after)

    def quarter(q):
        return pl.ds(pl.multiple_of(q * CELLS, CELLS), CELLS)

    def halo_out(q):
        if q == 3:
            return remote(
                planes_hbm.at[1, :, :, quarter(3)], planes.at[0, :, :, quarter(3)],
                halo_send.at[3], halo_recv.at[3], at(8, chan),
            )
        return remote(
            planes_hbm.at[1, :, :, quarter(q)], halo_relay,
            halo_send.at[q], h_recv, at(1 + 2 * q, chan),
        )

    halo_on = remote(
        halo_relay, planes.at[0, :, :, quarter(column)], h_send, halo_recv.at[column], at(8, chan)
    )
    load_even = pltpu.make_async_copy(planes_hbm.at[0], planes.at[1], local_sem.at[CHUNKS])
    load_odd = pltpu.make_async_copy(planes_hbm.at[1], planes.at[2], local_sem.at[CHUNKS + 1])

    def share_copy(k, q):
        return remote(share.at[k, q], share_in.at[k, q], p_send.at[k, q], p_recv.at[k, q], before)

    def share_out(k, q):
        if q == 0:
            return share_copy(k, 0)
        return remote(share.at[k, q], relay.at[k], p_send.at[k, q], q_recv.at[k], at(8 + 2 * q, chan))

    def share_on(k):
        return remote(relay.at[k], share_in.at[k, column], q_send.at[k], p_recv.at[k, column], at(7, chan))

    def send_share(k):
        @pl.when((slab > 0) & (slab != 8))
        def _():
            for q in range(4):
                share_copy(k, q).start()

        @pl.when(slab == 8)
        def _():
            for q in (1, 2, 3, 0):
                share_out(k, q).start()

    def pass_share(k):
        @pl.when(high_side)
        def _():
            share_out(k, 1).wait_recv()
            share_on(k).start()

    load_even.start()
    load_odd.start()
    for k in range(CHUNKS):
        local(k).start()

    is_edge = (slab == 7) | (slab == 8)
    is_side = low_side | high_side

    @pl.when(is_edge)
    def _():
        pl.semaphore_wait(barrier, len(peers) + 4)

    @pl.when(is_side)
    def _():
        pl.semaphore_wait(barrier, len(peers) + 1)

    @pl.when(jnp.logical_not(is_edge | is_side))
    def _():
        pl.semaphore_wait(barrier, len(peers))

    for copy in cross_y():
        copy.start()
    for k in range(4):
        for copy in z_copies(k):
            copy.start()

    @pl.when((slab < 15) & (slab != 7))
    def _():
        halo.start()

    @pl.when(slab == 7)
    def _():
        for q in range(4):
            halo_out(q).start()

    acc[...] = jnp.zeros_like(acc)
    load_even.wait()
    load_odd.wait()

    lane = lax.broadcasted_iota(jnp.int32, (8, CELLS), 1)
    first_col = lane % HALF == 0
    first_row = lane < HALF

    def view(depth_tap, sample, row_tap, col_tap):
        at_block = (2 * (row_tap != 1) + (col_tap != 1)) * CELLS
        v = planes[depth_tap, sample, :, at_block : at_block + CELLS].astype(jnp.float32)
        amount = (HALF if row_tap == 0 else 0) + (1 if col_tap == 0 else 0)
        if amount:
            v = pltpu.roll(v, amount, 1)
            drop = first_col if col_tap == 0 else first_row
            if col_tap == 0 and row_tap == 0:
                drop = first_col | first_row
            v = jnp.where(drop, 0.0, v)
        return v

    def fill(store, taps):
        for sample in range(2):
            for pair in range((len(taps) + 1) // 2):
                rows = []
                for t in taps[2 * pair : 2 * pair + 2]:
                    rows.append(view(t // 9, sample, (t // 3) % 3, t % 3))
                if len(rows) == 1:
                    rows.append(jnp.zeros_like(rows[0]))
                both = jnp.concatenate(rows, axis=0).astype(jnp.bfloat16)
                for j in range(PER_SAMPLE):
                    store[sample * PER_SAMPLE + PER_SAMPLE - 1 - j, 16 * pair : 16 * pair + 16, :] = both[
                        :, j * CHUNK : (j + 1) * CHUNK
                    ]

    def start_y(k):
        local(k).wait()
        for copy in z_copies(k):
            copy.wait_recv()
        for copy in y_copies(k):
            copy.start()

    def start_f(k):
        for copy in y_copies(k):
            copy.wait_recv()
        for copy in f_copies(k):
            copy.start()

    for copy in cross_y():
        copy.wait_recv()
    for copy in cross_f():
        copy.start()
    start_y(0)
    fill(early, EARLY)
    local(CROSS).wait()
    for copy in cross_f():
        copy.wait_recv()
    cross_send(0)

    chunk_lane = lax.broadcasted_iota(jnp.int32, (8, CHUNK), 1)
    last_col = chunk_lane % HALF == HALF - 1

    def row_ahead(value, tail):
        wide = jnp.concatenate([value, tail], axis=1)
        return pltpu.roll(wide, CHUNK + 128 - HALF, 1)[:, :CHUNK]

    def col_ahead(value):
        return jnp.where(last_col, 0.0, pltpu.roll(value, CHUNK - 1, 1))

    def phases(depth_tap):
        def fetch(row_tap, col_tap):
            row = 8 * (9 * depth_tap + 3 * row_tap + col_tap)
            return groups[row : row + 8, :]

        def odd_row(col_tap):
            at_carry = 3 * depth_tap + col_tap
            moving = fetch(0, col_tap)
            moved = row_ahead(moving, carry[at_carry])
            carry[at_carry] = moving[:, :128]
            return fetch(2, col_tap) + moved

        found = []
        rows_even = [fetch(1, c) for c in range(3)]
        rows_odd = [odd_row(c) for c in range(3)]
        for rows in (rows_even, rows_odd):
            found.append(rows[1])
            found.append(rows[2] + col_ahead(rows[0]))
        return found

    def lanes_of(k, phase):
        begin = phase * CELLS + (PER_SAMPLE - 1 - k % PER_SAMPLE) * CHUNK
        return pl.ds(pl.multiple_of(begin, CHUNK), CHUNK)

    def late_dot(k):
        term = lax.dot_general(
            held[k].reshape(256, CHUNK), late[k], (((1,), (1,)), ((), ())), preferred_element_type=jnp.float32
        )
        acc[:, :, :, :, 128:224] += term.reshape(2, 4, 2, 16, 96)

    def finish(k):
        @pl.when(slab < 15)
        def _():
            for q in range(4):
                share_copy(k, q).wait_recv()

        for phase in range(4):
            value = odd[k % 2, phase]
            inward = jnp.where(slab < 15, share_in[k, phase], 0.0)
            out_ref[1, k // PER_SAMPLE, :, lanes_of(k, phase)] = (value + inward).astype(jnp.bfloat16)

    def early_dot(k):
        term = lax.dot_general(
            held[k].reshape(256, CHUNK), early[k], (((1,), (1,)), ((), ())), preferred_element_type=jnp.float32
        )
        acc[:, :, :, :, :128] += term.reshape(2, 4, 2, 16, 128)

    def input_part(k):
        @pl.when(k % PER_SAMPLE == 0)
        def _():
            carry[...] = jnp.zeros_like(carry)

        groups[...] = jnp.dot(w_ref[...], held[k].reshape(256, CHUNK), preferred_element_type=jnp.float32)
        for phase, value in enumerate(phases(0)):
            share[k, phase] = value
        send_share(k)
        for phase, value in enumerate(phases(1)):
            out_ref[0, k // PER_SAMPLE, :, lanes_of(k, phase)] = value.astype(jnp.bfloat16)
        for phase, value in enumerate(phases(2)):
            odd[k % 2, phase] = value

    def receive(k):
        for copy in f_copies(k):
            copy.wait_recv()

    def step(k, _):
        @pl.when(k + 4 < CROSS)
        def _():
            for copy in z_copies(k + 4):
                copy.start()

        @pl.when(k + 2 < CROSS)
        def _():
            start_y(k + 2)

        start_f(k + 1)
        receive(k)
        input_part(k)
        early_dot(k)

        @pl.when(k == HALO_AT)
        def _():
            @pl.when((slab > 0) & (slab != 8))
            def _():
                halo.wait_recv()

            @pl.when(slab == 8)
            def _():
                for q in range(4):
                    pltpu.make_async_remote_copy(
                        src_ref=planes.at[0, :, :, quarter(q)], dst_ref=planes.at[0, :, :, quarter(q)],
                        send_sem=h_send, recv_sem=halo_recv.at[q], device_id=mirror, device_id_type=MESH,
                    ).wait_recv()

            @pl.when(slab == 0)
            def _():
                planes[0] = jnp.zeros_like(planes[0])

            fill(late, LATE)

            def catch_up(n, _):
                late_dot(n)
                return 0

            lax.fori_loop(0, HALO_AT, catch_up, 0)

        @pl.when(k == 1)
        def _():
            cross_recv(0)
            cross_send(1)

        @pl.when(k == 3)
        def _():
            cross_recv(1)
            cross_send(2)

        @pl.when(k == 1)
        def _():
            @pl.when(low_side)
            def _():
                halo_out(0).wait_recv()
                halo_on.start()

        @pl.when(k >= HALO_AT)
        def _():
            late_dot(k)

        @pl.when(k >= 1)
        def _():
            pass_share(k - 1)
            finish(k - 1)

        return 0

    start_y(1)
    start_f(0)
    lax.fori_loop(0, CROSS - 1, step, 0)

    tail = CROSS - 1
    pair_copy = remote(acc.at[:, :, 1 - core], pair_in, c_send, c_recv, pair)

    def spread(d):
        to = (place + d + 1) % 8
        return remote(paired.at[to // 4, to % 4], near.at[d], r_send.at[d], r_recv.at[d], spread_to[d])

    cross_recv(2)
    early_dot(CROSS)
    late_dot(CROSS)
    receive(tail)
    early_dot(tail)
    late_dot(tail)
    pair_copy.start()
    input_part(tail)
    pass_share(tail - 1)
    pair_copy.wait_recv()
    paired[...] = acc[:, :, core] + pair_in[...]
    for d in range(7):
        spread(d).start()
    finish(tail - 1)
    input_part(CROSS)
    pass_share(tail)
    finish(tail)
    pass_share(CROSS)
    finish(CROSS)
    total = paired[half, column]
    for d in range(7):
        spread(d).wait_recv()
        total = total + near[d]
    scale = 1.0 / math.sqrt(2 * 16 * CELLS)
    wg_ref[...] = total * scale

    pair_copy.wait_send()
    for d in range(7):
        spread(d).wait_send()
    for copy in cross_y() + cross_f():
        copy.wait_send()
    for hop in range(3):
        cross_wait_send(hop)

    def drain(k, _):
        @pl.when(k < CROSS)
        def _():
            for copy in z_copies(k) + y_copies(k) + f_copies(k):
                copy.wait_send()

        @pl.when(slab > 0)
        def _():
            for q in range(4):
                share_copy(k, q).wait_send()

        @pl.when(high_side)
        def _():
            share_on(k).wait_send()

        return 0

    lax.fori_loop(0, CHUNKS, drain, 0)

    @pl.when((slab < 15) & (slab != 7))
    def _():
        halo.wait_send()

    @pl.when(slab == 7)
    def _():
        for q in range(4):
            halo_out(q).wait_send()

    @pl.when(low_side)
    def _():
        halo_on.wait_send()


def body(activations, out_grad, weights):
    planes = activations.transpose(2, 0, 1, 3)
    grad = out_grad.reshape(2, 16, CELLS)
    w = weights.reshape(216, 256)
    sem = pltpu.SemaphoreType.DMA
    f32, bf16 = jnp.float32, jnp.bfloat16
    any_space = pl.BlockSpec(memory_space=pl.ANY)
    vmem = pl.BlockSpec(memory_space=pltpu.VMEM)
    out, wg = pl.pallas_call(
        gather_kernel,
        out_shape=(
            jax.ShapeDtypeStruct((2, 2, 8, 4 * CELLS), bf16),
            jax.ShapeDtypeStruct((16, 256), f32),
        ),
        in_specs=[any_space, any_space, vmem],
        out_specs=(vmem, vmem),
        scratch_shapes=[
            pltpu.VMEM((CHUNKS, 4, 4, 16, CHUNK), bf16),
            pltpu.VMEM((CHUNKS, 128, CHUNK), bf16),
            pltpu.VMEM((CHUNKS, 96, CHUNK), bf16),
            pltpu.VMEM((3, 2, 8, 4 * CELLS), bf16),
            pltpu.VMEM((216, CHUNK), f32),
            pltpu.VMEM((9, 8, 128), f32),
            pltpu.VMEM((CHUNKS, 4, 8, CHUNK), f32),
            pltpu.VMEM((CHUNKS, 4, 8, CHUNK), f32),
            pltpu.VMEM((2, 4, 8, CHUNK), f32),
            pltpu.VMEM((2, 4, 2, 16, 256), f32),
            pltpu.VMEM((2, 4, 16, 256), f32),
            pltpu.VMEM((2, 4, 16, 256), f32),
            pltpu.VMEM((7, 16, 256), f32),
            pltpu.VMEM((CHUNKS, 8, CHUNK), f32),
            pltpu.VMEM((2, 8, CELLS), bf16),
            sem((CHUNKS + 2,)),
            sem((CHUNKS, 3)), sem((CHUNKS, 3)),
            sem((CHUNKS, 2)), sem((CHUNKS, 2)),
            sem((CHUNKS, 2)), sem((CHUNKS, 2)),
            sem((4,)), sem((4,)),
            sem((CHUNKS, 4)), sem((CHUNKS, 4)),
            sem((CHUNKS,)), sem((CHUNKS,)),
            sem, sem,
            sem, sem,
            sem((7,)), sem((7,)),
            sem((2,)), sem((2,)),
            sem((2,)), sem((2,)),
            sem((2, 3)), sem((2, 3)),
        ],
        compiler_params=pltpu.CompilerParams(
            collective_id=0, has_side_effects=True, vmem_limit_bytes=48 * 1024 * 1024
        ),
    )(grad, planes, w)
    input_grad = out.transpose(1, 2, 0, 3)
    taps = wg[:, :216].reshape(16, 27, 8)
    taps = jnp.concatenate([taps[:, 18:], taps[:, :18]], axis=1)
    return input_grad, taps.transpose(1, 2, 0)


def solution(mesh):
    placed = (P(None, "chan", "slab", None), P(None, "chan", "slab", None), P(None, "chan", None))
    return jax.shard_map(
        body,
        mesh=mesh,
        in_specs=placed,
        out_specs=(P(None, "chan", "slab", None), P(None, "chan", "slab")),
        check_vma=False,
    )
```

```python
import functools
import math

import jax
import jax.numpy as jnp
from jax import lax
from jax.experimental import pallas as pl
from jax.experimental.pallas import tpu as pltpu
from jax.sharding import PartitionSpec as P

MESH = pl.DeviceIdType.MESH
EDGE = 128
HALF = EDGE // 2
CELLS = HALF * HALF
CHUNK = 1024
PER_SAMPLE = CELLS // CHUNK
CHUNKS = 2 * PER_SAMPLE
EARLY = tuple(range(9, 25))
HALO_AT = 4
AHEAD = 4
CROSS = CHUNKS - 1
LATE = (25, 26) + tuple(range(9))


def gather_kernel(
    grad_hbm, planes_hbm, w_ref, out_ref, wg_ref,
    held, early, late, planes, groups, carry, share, share_in,
    odd, acc, pair_in, paired, near, relay, halo_relay,
    local_sem, z_send, z_recv, o_send, o_recv, y_send, y_recv, f_send, f_recv,
    halo_send, halo_recv, p_send, p_recv, q_send, q_recv, h_send, h_recv,
    c_send, c_recv, r_send, r_recv, bf_send, bf_recv, bz_send, bz_recv,
):
    slab = lax.axis_index("slab")
    chan = lax.axis_index("chan")
    y, z = chan // 4, chan % 4
    half, spot = slab // 8, slab % 8

    def at(slab_to, chan_to):
        return (slab_to, chan_to)

    along_z = [at(slab, y * 4 + (z + d) % 4) for d in range(1, 4)]
    y_up = at(slab, ((y + 1) % 4) * 4 + z)
    y_down = at(slab, ((y + 3) % 4) * 4 + z)
    column, core = spot // 2, spot % 2
    near_to = [at(half * 8 + (spot + d) % 8, chan) for d in range(1, 8)]
    pair = at(slab + 1 - 2 * core, chan)
    place = half * 4 + column

    def core_peer(d):
        to = (place + d) % 8
        return at((to // 4) * 8 + (to % 4) * 2 + core, chan)

    spread_to = [core_peer(d) for d in range(1, 8)]
    across = [at((1 - half) * 8 + (spot + 2 * d) % 8, chan) for d in range(4)]
    mirror = at((1 - half) * 8 + spot, chan)
    before = at(lax.max(slab - 1, 0), chan)
    after = at(lax.min(slab + 1, 15), chan)
    low_side = (slab < 6) & (core == 1)
    high_side = (slab > 8) & (core == 0)

    barrier = pltpu.get_barrier_semaphore()
    peers = along_z + [y_up, y_down] + near_to + across

    def greet(peer):
        pl.semaphore_signal(barrier, inc=1, device_id=peer, device_id_type=MESH)

    for peer in peers:
        greet(peer)

    @pl.when(slab == 7)
    def _():
        for q in range(4):
            greet(at(8 + 2 * q, chan))

    @pl.when(slab == 8)
    def _():
        for q in range(4):
            greet(at(1 + 2 * q, chan))

    @pl.when(low_side)
    def _():
        greet(at(8, chan))

    @pl.when(high_side)
    def _():
        greet(at(7, chan))

    def source(k):
        begin = pl.multiple_of((PER_SAMPLE - 1 - k % PER_SAMPLE) * CHUNK, CHUNK)
        return grad_hbm.at[k // PER_SAMPLE, :, pl.ds(begin, CHUNK)]

    def local(k):
        return pltpu.make_async_copy(source(k), held.at[k, y, z], local_sem.at[k])

    def remote(src, dst, send, recv, to):
        return pltpu.make_async_remote_copy(
            src_ref=src, dst_ref=dst, send_sem=send, recv_sem=recv, device_id=to, device_id_type=MESH
        )

    def z_copies(k):
        return [
            remote(source(k), held.at[k, y, z], z_send.at[k, d], z_recv.at[k, d], along_z[d])
            for d in range(3)
        ]

    low, high = (y + 3) % 4, (y + 1) % 4

    def y_own(k):
        return [
            remote(source(k), held.at[k, y, z], o_send.at[k, 0], o_recv.at[k, 0], y_up),
            remote(source(k), held.at[k, y, z], o_send.at[k, 1], o_recv.at[k, 1], y_down),
        ]

    def y_piece(k, d):
        piece = held.at[k, y, (z + 3 - d) % 4]
        return [
            remote(piece, piece, y_send.at[k, d, 0], y_recv.at[k, d, 0], y_up),
            remote(piece, piece, y_send.at[k, d, 1], y_recv.at[k, d, 1], y_down),
        ]

    def y_copies(k):
        return y_own(k) + y_piece(k, 0) + y_piece(k, 1) + y_piece(k, 2)

    def f_copies(k):
        from_low, from_high = held.at[k, low, pl.ds(0, 2)], held.at[k, high, pl.ds(2, 2)]
        return [
            remote(from_low, from_low, f_send.at[k, 0], f_recv.at[k, 0], y_up),
            remote(from_high, from_high, f_send.at[k, 1], f_recv.at[k, 1], y_down),
        ]

    def cross_y():
        return y_own(CROSS)

    def cross_f():
        from_low = held.at[CROSS, low, z, :, pl.ds(0, CHUNK // 2)]
        from_high = held.at[CROSS, high, z, :, pl.ds(CHUNK // 2, CHUNK // 2)]
        return [
            remote(from_low, from_low, bf_send.at[0], bf_recv.at[0], y_up),
            remote(from_high, from_high, bf_send.at[1], bf_recv.at[1], y_down),
        ]

    z_up = at(slab, y * 4 + lax.min(z + 1, 3))
    z_down = at(slab, y * 4 + lax.max(z - 1, 0))

    def cross_up(hop):
        piece = held.at[CROSS, :, lax.max(z - hop, 0)]
        return remote(piece, piece, bz_send.at[0, hop], bz_recv.at[0, hop], z_up)

    def cross_down(hop):
        piece = held.at[CROSS, :, lax.min(z + hop, 3)]
        return remote(piece, piece, bz_send.at[1, hop], bz_recv.at[1, hop], z_down)

    def cross_send(hop):
        @pl.when((z < 3) & (z >= hop))
        def _():
            cross_up(hop).start()

        @pl.when((z > 0) & (z + hop <= 3))
        def _():
            cross_down(hop).start()

    def cross_wait_send(hop):
        @pl.when((z < 3) & (z >= hop))
        def _():
            cross_up(hop).wait_send()

        @pl.when((z > 0) & (z + hop <= 3))
        def _():
            cross_down(hop).wait_send()

    def cross_recv(hop):
        @pl.when(z > hop)
        def _():
            cross_up(hop).wait_recv()

        @pl.when(z + hop < 3)
        def _():
            cross_down(hop).wait_recv()

    halo = remote(planes_hbm.at[1], planes.at[0], halo_send.at[0], halo_recv.at[0], after)

    def quarter(q):
        return pl.ds(pl.multiple_of(q * CELLS, CELLS), CELLS)

    def halo_out(q):
        if q == 3:
            return remote(
                planes_hbm.at[1, :, :, quarter(3)], planes.at[0, :, :, quarter(3)],
                halo_send.at[3], halo_recv.at[3], at(8, chan),
            )
        return remote(
            planes_hbm.at[1, :, :, quarter(q)], halo_relay,
            halo_send.at[q], h_recv, at(1 + 2 * q, chan),
        )

    halo_on = remote(
        halo_relay, planes.at[0, :, :, quarter(column)], h_send, halo_recv.at[column], at(8, chan)
    )
    load_even = pltpu.make_async_copy(planes_hbm.at[0], planes.at[1], local_sem.at[CHUNKS])
    load_odd = pltpu.make_async_copy(planes_hbm.at[1], planes.at[2], local_sem.at[CHUNKS + 1])

    def share_copy(k, q):
        return remote(share.at[k, q], share_in.at[k, q], p_send.at[k, q], p_recv.at[k, q], before)

    def share_out(k, q):
        if q == 0:
            return share_copy(k, 0)
        return remote(share.at[k, q], relay.at[k], p_send.at[k, q], q_recv.at[k], at(8 + 2 * q, chan))

    def share_on(k):
        return remote(relay.at[k], share_in.at[k, column], q_send.at[k], p_recv.at[k, column], at(7, chan))

    def send_share(k):
        @pl.when((slab > 0) & (slab != 8))
        def _():
            for q in range(4):
                share_copy(k, q).start()

        @pl.when(slab == 8)
        def _():
            for q in (1, 2, 3, 0):
                share_out(k, q).start()

    def pass_share(k):
        @pl.when(high_side)
        def _():
            share_out(k, 1).wait_recv()
            share_on(k).start()

    load_even.start()
    load_odd.start()
    for k in range(CHUNKS):
        local(k).start()

    is_edge = (slab == 7) | (slab == 8)
    is_side = low_side | high_side

    @pl.when(is_edge)
    def _():
        pl.semaphore_wait(barrier, len(peers) + 4)

    @pl.when(is_side)
    def _():
        pl.semaphore_wait(barrier, len(peers) + 1)

    @pl.when(jnp.logical_not(is_edge | is_side))
    def _():
        pl.semaphore_wait(barrier, len(peers))

    for copy in z_copies(0) + cross_y():
        copy.start()
    for k in range(CROSS):
        for copy in y_own(k) + (z_copies(k) if 0 < k < AHEAD else []):
            copy.start()

    @pl.when((slab < 15) & (slab != 7))
    def _():
        halo.start()

    @pl.when(slab == 7)
    def _():
        for q in range(4):
            halo_out(q).start()

    acc[...] = jnp.zeros_like(acc)
    load_even.wait()
    load_odd.wait()

    lane = lax.broadcasted_iota(jnp.int32, (8, CELLS), 1)
    first_col = lane % HALF == 0
    first_row = lane < HALF

    def view(depth_tap, sample, row_tap, col_tap):
        at_block = (2 * (row_tap != 1) + (col_tap != 1)) * CELLS
        v = planes[depth_tap, sample, :, at_block : at_block + CELLS].astype(jnp.float32)
        amount = (HALF if row_tap == 0 else 0) + (1 if col_tap == 0 else 0)
        if amount:
            v = pltpu.roll(v, amount, 1)
            drop = first_col if col_tap == 0 else first_row
            if col_tap == 0 and row_tap == 0:
                drop = first_col | first_row
            v = jnp.where(drop, 0.0, v)
        return v

    def fill(store, taps):
        for sample in range(2):
            for pair in range((len(taps) + 1) // 2):
                rows = []
                for t in taps[2 * pair : 2 * pair + 2]:
                    rows.append(view(t // 9, sample, (t // 3) % 3, t % 3))
                if len(rows) == 1:
                    rows.append(jnp.zeros_like(rows[0]))
                both = jnp.concatenate(rows, axis=0).astype(jnp.bfloat16)
                for j in range(PER_SAMPLE):
                    store[sample * PER_SAMPLE + PER_SAMPLE - 1 - j, 16 * pair : 16 * pair + 16, :] = both[
                        :, j * CHUNK : (j + 1) * CHUNK
                    ]

    def start_y(k):
        for d, copy in enumerate(z_copies(k)):
            copy.wait_recv()
            for onward in y_piece(k, d):
                onward.start()

    def start_f(k):
        for copy in y_copies(k):
            copy.wait_recv()
        for copy in f_copies(k):
            copy.start()

    for copy in cross_y():
        copy.wait_recv()
    for copy in cross_f():
        copy.start()
    start_y(0)
    fill(early, EARLY)
    local(CROSS).wait()
    for copy in cross_f():
        copy.wait_recv()
    cross_send(0)

    chunk_lane = lax.broadcasted_iota(jnp.int32, (8, CHUNK), 1)
    last_col = chunk_lane % HALF == HALF - 1

    def row_ahead(value, tail):
        wide = jnp.concatenate([value, tail], axis=1)
        return pltpu.roll(wide, CHUNK + 128 - HALF, 1)[:, :CHUNK]

    def col_ahead(value):
        return jnp.where(last_col, 0.0, pltpu.roll(value, CHUNK - 1, 1))

    def phases(depth_tap):
        def fetch(row_tap, col_tap):
            row = 8 * (9 * depth_tap + 3 * row_tap + col_tap)
            return groups[row : row + 8, :]

        def odd_row(col_tap):
            at_carry = 3 * depth_tap + col_tap
            moving = fetch(0, col_tap)
            moved = row_ahead(moving, carry[at_carry])
            carry[at_carry] = moving[:, :128]
            return fetch(2, col_tap) + moved

        found = []
        rows_even = [fetch(1, c) for c in range(3)]
        rows_odd = [odd_row(c) for c in range(3)]
        for rows in (rows_even, rows_odd):
            found.append(rows[1])
            found.append(rows[2] + col_ahead(rows[0]))
        return found

    def lanes_of(k, phase):
        begin = phase * CELLS + (PER_SAMPLE - 1 - k % PER_SAMPLE) * CHUNK
        return pl.ds(pl.multiple_of(begin, CHUNK), CHUNK)

    def late_dot(k):
        term = lax.dot_general(
            held[k].reshape(256, CHUNK), late[k], (((1,), (1,)), ((), ())), preferred_element_type=jnp.float32
        )
        acc[:, :, :, :, 128:224] += term.reshape(2, 4, 2, 16, 96)

    def finish(k):
        @pl.when(slab < 15)
        def _():
            for q in range(4):
                share_copy(k, q).wait_recv()

        for phase in range(4):
            value = odd[k % 2, phase]
            inward = jnp.where(slab < 15, share_in[k, phase], 0.0)
            out_ref[1, k // PER_SAMPLE, :, lanes_of(k, phase)] = (value + inward).astype(jnp.bfloat16)

    def early_dot(k):
        term = lax.dot_general(
            held[k].reshape(256, CHUNK), early[k], (((1,), (1,)), ((), ())), preferred_element_type=jnp.float32
        )
        acc[:, :, :, :, :128] += term.reshape(2, 4, 2, 16, 128)

    def input_part(k):
        @pl.when(k % PER_SAMPLE == 0)
        def _():
            carry[...] = jnp.zeros_like(carry)

        groups[...] = jnp.dot(w_ref[...], held[k].reshape(256, CHUNK), preferred_element_type=jnp.float32)
        for phase, value in enumerate(phases(0)):
            share[k, phase] = value
        send_share(k)
        for phase, value in enumerate(phases(1)):
            out_ref[0, k // PER_SAMPLE, :, lanes_of(k, phase)] = value.astype(jnp.bfloat16)
        for phase, value in enumerate(phases(2)):
            odd[k % 2, phase] = value

    def receive(k):
        local(k).wait()
        for copy in f_copies(k):
            copy.wait_recv()

    def step(k, _):
        @pl.when(k + AHEAD < CROSS)
        def _():
            for copy in z_copies(k + AHEAD):
                copy.start()

        @pl.when(k + 2 < CROSS)
        def _():
            start_y(k + 2)

        start_f(k + 1)
        receive(k)
        input_part(k)
        early_dot(k)

        @pl.when(k == HALO_AT)
        def _():
            @pl.when((slab > 0) & (slab != 8))
            def _():
                halo.wait_recv()

            @pl.when(slab == 8)
            def _():
                for q in range(4):
                    pltpu.make_async_remote_copy(
                        src_ref=planes.at[0, :, :, quarter(q)], dst_ref=planes.at[0, :, :, quarter(q)],
                        send_sem=h_send, recv_sem=halo_recv.at[q], device_id=mirror, device_id_type=MESH,
                    ).wait_recv()

            @pl.when(slab == 0)
            def _():
                planes[0] = jnp.zeros_like(planes[0])

            fill(late, LATE)

            def catch_up(n, _):
                late_dot(n)
                return 0

            lax.fori_loop(0, HALO_AT, catch_up, 0)

        @pl.when(k == 1)
        def _():
            cross_recv(0)
            cross_send(1)

        @pl.when(k == 3)
        def _():
            cross_recv(1)
            cross_send(2)

        @pl.when(k == 1)
        def _():
            @pl.when(low_side)
            def _():
                halo_out(0).wait_recv()
                halo_on.start()

        @pl.when(k >= HALO_AT)
        def _():
            late_dot(k)

        @pl.when(k >= 1)
        def _():
            pass_share(k - 1)
            finish(k - 1)

        return 0

    start_y(1)
    start_f(0)
    lax.fori_loop(0, CROSS - 1, step, 0)

    tail = CROSS - 1
    pair_copy = remote(acc.at[:, :, 1 - core], pair_in, c_send, c_recv, pair)

    def spread(d):
        to = (place + d + 1) % 8
        return remote(paired.at[to // 4, to % 4], near.at[d], r_send.at[d], r_recv.at[d], spread_to[d])

    cross_recv(2)
    early_dot(CROSS)
    late_dot(CROSS)
    receive(tail)
    early_dot(tail)
    late_dot(tail)
    pair_copy.start()
    input_part(tail)
    pass_share(tail - 1)
    pair_copy.wait_recv()
    paired[...] = acc[:, :, core] + pair_in[...]
    for d in range(7):
        spread(d).start()
    finish(tail - 1)
    input_part(CROSS)
    pass_share(tail)
    finish(tail)
    pass_share(CROSS)
    finish(CROSS)
    total = paired[half, column]
    for d in range(7):
        spread(d).wait_recv()
        total = total + near[d]
    scale = 1.0 / math.sqrt(2 * 16 * CELLS)
    wg_ref[...] = total * scale

    pair_copy.wait_send()
    for d in range(7):
        spread(d).wait_send()
    for copy in cross_y() + cross_f():
        copy.wait_send()
    for hop in range(3):
        cross_wait_send(hop)

    def drain(k, _):
        @pl.when(k < CROSS)
        def _():
            for copy in z_copies(k) + y_copies(k) + f_copies(k):
                copy.wait_send()

        @pl.when(slab > 0)
        def _():
            for q in range(4):
                share_copy(k, q).wait_send()

        @pl.when(high_side)
        def _():
            share_on(k).wait_send()

        return 0

    lax.fori_loop(0, CHUNKS, drain, 0)

    @pl.when((slab < 15) & (slab != 7))
    def _():
        halo.wait_send()

    @pl.when(slab == 7)
    def _():
        for q in range(4):
            halo_out(q).wait_send()

    @pl.when(low_side)
    def _():
        halo_on.wait_send()


def body(activations, out_grad, weights):
    planes = activations.transpose(2, 0, 1, 3)
    grad = out_grad.reshape(2, 16, CELLS)
    w = weights.reshape(216, 256)
    sem = pltpu.SemaphoreType.DMA
    f32, bf16 = jnp.float32, jnp.bfloat16
    any_space = pl.BlockSpec(memory_space=pl.ANY)
    vmem = pl.BlockSpec(memory_space=pltpu.VMEM)
    out, wg = pl.pallas_call(
        gather_kernel,
        out_shape=(
            jax.ShapeDtypeStruct((2, 2, 8, 4 * CELLS), bf16),
            jax.ShapeDtypeStruct((16, 256), f32),
        ),
        in_specs=[any_space, any_space, vmem],
        out_specs=(vmem, vmem),
        scratch_shapes=[
            pltpu.VMEM((CHUNKS, 4, 4, 16, CHUNK), bf16),
            pltpu.VMEM((CHUNKS, 128, CHUNK), bf16),
            pltpu.VMEM((CHUNKS, 96, CHUNK), bf16),
            pltpu.VMEM((3, 2, 8, 4 * CELLS), bf16),
            pltpu.VMEM((216, CHUNK), f32),
            pltpu.VMEM((9, 8, 128), f32),
            pltpu.VMEM((CHUNKS, 4, 8, CHUNK), f32),
            pltpu.VMEM((CHUNKS, 4, 8, CHUNK), f32),
            pltpu.VMEM((2, 4, 8, CHUNK), f32),
            pltpu.VMEM((2, 4, 2, 16, 256), f32),
            pltpu.VMEM((2, 4, 16, 256), f32),
            pltpu.VMEM((2, 4, 16, 256), f32),
            pltpu.VMEM((7, 16, 256), f32),
            pltpu.VMEM((CHUNKS, 8, CHUNK), f32),
            pltpu.VMEM((2, 8, CELLS), bf16),
            sem((CHUNKS + 2,)),
            sem((CHUNKS, 3)), sem((CHUNKS, 3)),
            sem((CHUNKS, 2)), sem((CHUNKS, 2)),
            sem((CHUNKS, 3, 2)), sem((CHUNKS, 3, 2)),
            sem((CHUNKS, 2)), sem((CHUNKS, 2)),
            sem((4,)), sem((4,)),
            sem((CHUNKS, 4)), sem((CHUNKS, 4)),
            sem((CHUNKS,)), sem((CHUNKS,)),
            sem, sem,
            sem, sem,
            sem((7,)), sem((7,)),
            sem((2,)), sem((2,)),
            sem((2, 3)), sem((2, 3)),
        ],
        compiler_params=pltpu.CompilerParams(
            collective_id=0, has_side_effects=True, vmem_limit_bytes=48 * 1024 * 1024
        ),
    )(grad, planes, w)
    input_grad = out.transpose(1, 2, 0, 3)
    taps = wg[:, :216].reshape(16, 27, 8)
    taps = jnp.concatenate([taps[:, 18:], taps[:, :18]], axis=1)
    return input_grad, taps.transpose(1, 2, 0)


def solution(mesh):
    placed = (P(None, "chan", "slab", None), P(None, "chan", "slab", None), P(None, "chan", None))
    return jax.shard_map(
        body,
        mesh=mesh,
        in_specs=placed,
        out_specs=(P(None, "chan", "slab", None), P(None, "chan", "slab")),
        check_vma=False,
    )
```

```python
import functools
import math

import jax
import jax.numpy as jnp
from jax import lax
from jax.experimental import pallas as pl
from jax.experimental.pallas import tpu as pltpu
from jax.sharding import PartitionSpec as P

MESH = pl.DeviceIdType.MESH
EDGE = 128
HALF = EDGE // 2
CELLS = HALF * HALF
CHUNK = 1024
PER_SAMPLE = CELLS // CHUNK
CHUNKS = 2 * PER_SAMPLE
EARLY = tuple(range(9, 25))
HALO_AT = 4
AHEAD = 4
CROSS = CHUNKS - 1
LATE = (25, 26) + tuple(range(9))


def gather_kernel(
    grad_hbm, planes_hbm, w_ref, out_ref, wg_ref,
    held, early, late, planes, groups, carry, share, share_in,
    odd, acc, pair_in, paired, near, relay, halo_relay,
    local_sem, z_send, z_recv, o_send, o_recv, y_send, y_recv, f_send, f_recv,
    halo_send, halo_recv, p_send, p_recv, q_send, q_recv, h_send, h_recv,
    c_send, c_recv, r_send, r_recv, bf_send, bf_recv, bz_send, bz_recv,
):
    slab = lax.axis_index("slab")
    chan = lax.axis_index("chan")
    y, z = chan // 4, chan % 4
    half, spot = slab // 8, slab % 8

    def at(slab_to, chan_to):
        return (slab_to, chan_to)

    along_z = [at(slab, y * 4 + (z + d) % 4) for d in range(1, 4)]
    y_up = at(slab, ((y + 1) % 4) * 4 + z)
    y_down = at(slab, ((y + 3) % 4) * 4 + z)
    column, core = spot // 2, spot % 2
    near_to = [at(half * 8 + (spot + d) % 8, chan) for d in range(1, 8)]
    pair = at(slab + 1 - 2 * core, chan)
    place = half * 4 + column

    def core_peer(d):
        to = (place + d) % 8
        return at((to // 4) * 8 + (to % 4) * 2 + core, chan)

    spread_to = [core_peer(d) for d in range(1, 8)]
    across = [at((1 - half) * 8 + (spot + 2 * d) % 8, chan) for d in range(4)]
    mirror = at((1 - half) * 8 + spot, chan)
    before = at(lax.max(slab - 1, 0), chan)
    after = at(lax.min(slab + 1, 15), chan)
    low_side = (slab < 6) & (core == 1)
    high_side = (slab > 8) & (core == 0)

    barrier = pltpu.get_barrier_semaphore()
    peers = along_z + [y_up, y_down] + near_to + across

    def greet(peer):
        pl.semaphore_signal(barrier, inc=1, device_id=peer, device_id_type=MESH)

    for peer in peers:
        greet(peer)

    @pl.when(slab == 7)
    def _():
        for q in range(4):
            greet(at(8 + 2 * q, chan))

    @pl.when(slab == 8)
    def _():
        for q in range(4):
            greet(at(1 + 2 * q, chan))

    @pl.when(low_side)
    def _():
        greet(at(8, chan))

    @pl.when(high_side)
    def _():
        greet(at(7, chan))

    def sample_of(k):
        return ((k + 1) // PER_SAMPLE) % 2

    def begin_of(k):
        later = min(k // 3, 1) if isinstance(k, int) else lax.min(k // 3, 1)
        return (PER_SAMPLE - 1 - k + 3 * later + k // CROSS) * CHUNK

    def slot_of(k):
        return k % 2 + k // CROSS

    def source(k):
        return grad_hbm.at[sample_of(k), :, pl.ds(pl.multiple_of(begin_of(k), CHUNK), CHUNK)]

    def local(k):
        return pltpu.make_async_copy(source(k), held.at[k, y, z], local_sem.at[k])

    def remote(src, dst, send, recv, to):
        return pltpu.make_async_remote_copy(
            src_ref=src, dst_ref=dst, send_sem=send, recv_sem=recv, device_id=to, device_id_type=MESH
        )

    def z_copies(k):
        return [
            remote(source(k), held.at[k, y, z], z_send.at[k, d], z_recv.at[k, d], along_z[d])
            for d in range(3)
        ]

    low, high = (y + 3) % 4, (y + 1) % 4

    def y_own(k):
        return [
            remote(source(k), held.at[k, y, z], o_send.at[k, 0], o_recv.at[k, 0], y_up),
            remote(source(k), held.at[k, y, z], o_send.at[k, 1], o_recv.at[k, 1], y_down),
        ]

    def y_piece(k, d):
        piece = held.at[k, y, (z + 3 - d) % 4]
        return [
            remote(piece, piece, y_send.at[k, d, 0], y_recv.at[k, d, 0], y_up),
            remote(piece, piece, y_send.at[k, d, 1], y_recv.at[k, d, 1], y_down),
        ]

    def y_copies(k):
        return y_own(k) + y_piece(k, 0) + y_piece(k, 1) + y_piece(k, 2)

    def f_copies(k):
        from_low, from_high = held.at[k, low, pl.ds(0, 2)], held.at[k, high, pl.ds(2, 2)]
        return [
            remote(from_low, from_low, f_send.at[k, 0], f_recv.at[k, 0], y_up),
            remote(from_high, from_high, f_send.at[k, 1], f_recv.at[k, 1], y_down),
        ]

    def cross_y():
        return y_own(CROSS)

    def cross_f():
        from_low = held.at[CROSS, low, z, :, pl.ds(0, CHUNK // 2)]
        from_high = held.at[CROSS, high, z, :, pl.ds(CHUNK // 2, CHUNK // 2)]
        return [
            remote(from_low, from_low, bf_send.at[0], bf_recv.at[0], y_up),
            remote(from_high, from_high, bf_send.at[1], bf_recv.at[1], y_down),
        ]

    z_up = at(slab, y * 4 + lax.min(z + 1, 3))
    z_down = at(slab, y * 4 + lax.max(z - 1, 0))

    def cross_up(hop):
        piece = held.at[CROSS, :, lax.max(z - hop, 0)]
        return remote(piece, piece, bz_send.at[0, hop], bz_recv.at[0, hop], z_up)

    def cross_down(hop):
        piece = held.at[CROSS, :, lax.min(z + hop, 3)]
        return remote(piece, piece, bz_send.at[1, hop], bz_recv.at[1, hop], z_down)

    def cross_send(hop):
        @pl.when((z < 3) & (z >= hop))
        def _():
            cross_up(hop).start()

        @pl.when((z > 0) & (z + hop <= 3))
        def _():
            cross_down(hop).start()

    def cross_wait_send(hop):
        @pl.when((z < 3) & (z >= hop))
        def _():
            cross_up(hop).wait_send()

        @pl.when((z > 0) & (z + hop <= 3))
        def _():
            cross_down(hop).wait_send()

    def cross_recv(hop):
        @pl.when(z > hop)
        def _():
            cross_up(hop).wait_recv()

        @pl.when(z + hop < 3)
        def _():
            cross_down(hop).wait_recv()

    halo = remote(planes_hbm.at[1], planes.at[0], halo_send.at[0], halo_recv.at[0], after)

    def quarter(q):
        return pl.ds(pl.multiple_of(q * CELLS, CELLS), CELLS)

    def halo_out(q):
        if q == 3:
            return remote(
                planes_hbm.at[1, :, :, quarter(3)], planes.at[0, :, :, quarter(3)],
                halo_send.at[3], halo_recv.at[3], at(8, chan),
            )
        return remote(
            planes_hbm.at[1, :, :, quarter(q)], halo_relay,
            halo_send.at[q], h_recv, at(1 + 2 * q, chan),
        )

    halo_on = remote(
        halo_relay, planes.at[0, :, :, quarter(column)], h_send, halo_recv.at[column], at(8, chan)
    )
    load_even = pltpu.make_async_copy(planes_hbm.at[0], planes.at[1], local_sem.at[CHUNKS])
    load_odd = pltpu.make_async_copy(planes_hbm.at[1], planes.at[2], local_sem.at[CHUNKS + 1])

    def share_copy(k, q):
        return remote(share.at[k, q], share_in.at[k, q], p_send.at[k, q], p_recv.at[k, q], before)

    def share_out(k, q):
        if q == 0:
            return share_copy(k, 0)
        return remote(share.at[k, q], relay.at[k], p_send.at[k, q], q_recv.at[k], at(8 + 2 * q, chan))

    def share_on(k):
        return remote(relay.at[k], share_in.at[k, column], q_send.at[k], p_recv.at[k, column], at(7, chan))

    def send_share(k):
        @pl.when((slab > 0) & (slab != 8))
        def _():
            for q in range(4):
                share_copy(k, q).start()

        @pl.when(slab == 8)
        def _():
            for q in (1, 2, 3, 0):
                share_out(k, q).start()

    def pass_share(k):
        @pl.when(high_side)
        def _():
            share_out(k, 1).wait_recv()
            share_on(k).start()

    load_even.start()
    load_odd.start()
    for k in range(CHUNKS):
        local(k).start()

    is_edge = (slab == 7) | (slab == 8)
    is_side = low_side | high_side

    @pl.when(is_edge)
    def _():
        pl.semaphore_wait(barrier, len(peers) + 4)

    @pl.when(is_side)
    def _():
        pl.semaphore_wait(barrier, len(peers) + 1)

    @pl.when(jnp.logical_not(is_edge | is_side))
    def _():
        pl.semaphore_wait(barrier, len(peers))

    for copy in z_copies(0) + cross_y():
        copy.start()
    for k in range(CROSS):
        for copy in y_own(k) + (z_copies(k) if 0 < k < AHEAD else []):
            copy.start()

    @pl.when((slab < 15) & (slab != 7))
    def _():
        halo.start()

    @pl.when(slab == 7)
    def _():
        for q in range(4):
            halo_out(q).start()

    acc[...] = jnp.zeros_like(acc)
    carry[...] = jnp.zeros_like(carry)
    load_even.wait()
    load_odd.wait()

    lane = lax.broadcasted_iota(jnp.int32, (8, CELLS), 1)
    first_col = lane % HALF == 0
    first_row = lane < HALF

    def view(depth_tap, sample, row_tap, col_tap):
        at_block = (2 * (row_tap != 1) + (col_tap != 1)) * CELLS
        v = planes[depth_tap, sample, :, at_block : at_block + CELLS].astype(jnp.float32)
        amount = (HALF if row_tap == 0 else 0) + (1 if col_tap == 0 else 0)
        if amount:
            v = pltpu.roll(v, amount, 1)
            drop = first_col if col_tap == 0 else first_row
            if col_tap == 0 and row_tap == 0:
                drop = first_col | first_row
            v = jnp.where(drop, 0.0, v)
        return v

    def fill(store, taps):
        for sample in range(2):
            for pair in range((len(taps) + 1) // 2):
                rows = []
                for t in taps[2 * pair : 2 * pair + 2]:
                    rows.append(view(t // 9, sample, (t // 3) % 3, t % 3))
                if len(rows) == 1:
                    rows.append(jnp.zeros_like(rows[0]))
                both = jnp.concatenate(rows, axis=0).astype(jnp.bfloat16)
                for j in range(PER_SAMPLE):
                    k = 6 - j if sample else (CROSS if j == 0 else 3 - j)
                    store[k, 16 * pair : 16 * pair + 16, :] = both[
                        :, j * CHUNK : (j + 1) * CHUNK
                    ]

    def start_y(k):
        for d, copy in enumerate(z_copies(k)):
            copy.wait_recv()
            for onward in y_piece(k, d):
                onward.start()

    def start_f(k):
        for copy in y_copies(k):
            copy.wait_recv()
        for copy in f_copies(k):
            copy.start()

    for copy in cross_y():
        copy.wait_recv()
    for copy in cross_f():
        copy.start()
    start_y(0)
    fill(early, EARLY)
    local(CROSS).wait()
    for copy in cross_f():
        copy.wait_recv()
    cross_send(0)

    chunk_lane = lax.broadcasted_iota(jnp.int32, (8, CHUNK), 1)
    last_col = chunk_lane % HALF == HALF - 1

    def row_ahead(value, tail):
        wide = jnp.concatenate([value, tail], axis=1)
        return pltpu.roll(wide, CHUNK + 128 - HALF, 1)[:, :CHUNK]

    def col_ahead(value):
        return jnp.where(last_col, 0.0, pltpu.roll(value, CHUNK - 1, 1))

    def phases(depth_tap, sample):
        def fetch(row_tap, col_tap):
            row = 8 * (9 * depth_tap + 3 * row_tap + col_tap)
            return groups[row : row + 8, :]

        def odd_row(col_tap):
            at_carry = sample, 3 * depth_tap + col_tap
            moving = fetch(0, col_tap)
            moved = row_ahead(moving, carry[at_carry])
            carry[at_carry] = moving[:, :128]
            return fetch(2, col_tap) + moved

        found = []
        rows_even = [fetch(1, c) for c in range(3)]
        rows_odd = [odd_row(c) for c in range(3)]
        for rows in (rows_even, rows_odd):
            found.append(rows[1])
            found.append(rows[2] + col_ahead(rows[0]))
        return found

    def lanes_of(k, phase):
        return pl.ds(pl.multiple_of(phase * CELLS + begin_of(k), CHUNK), CHUNK)

    def late_dot(k):
        term = lax.dot_general(
            held[k].reshape(256, CHUNK), late[k], (((1,), (1,)), ((), ())), preferred_element_type=jnp.float32
        )
        acc[:, :, :, :, 128:224] += term.reshape(2, 4, 2, 16, 96)

    def finish(k):
        @pl.when(slab < 15)
        def _():
            for q in range(4):
                share_copy(k, q).wait_recv()

        for phase in range(4):
            value = odd[slot_of(k), phase]
            inward = jnp.where(slab < 15, share_in[k, phase], 0.0)
            out_ref[1, sample_of(k), :, lanes_of(k, phase)] = (value + inward).astype(jnp.bfloat16)

    def early_dot(k):
        term = lax.dot_general(
            held[k].reshape(256, CHUNK), early[k], (((1,), (1,)), ((), ())), preferred_element_type=jnp.float32
        )
        acc[:, :, :, :, :128] += term.reshape(2, 4, 2, 16, 128)

    def input_part(k):
        groups[...] = jnp.dot(w_ref[...], held[k].reshape(256, CHUNK), preferred_element_type=jnp.float32)
        for phase, value in enumerate(phases(0, sample_of(k))):
            share[k, phase] = value
        send_share(k)
        for phase, value in enumerate(phases(1, sample_of(k))):
            out_ref[0, sample_of(k), :, lanes_of(k, phase)] = value.astype(jnp.bfloat16)
        for phase, value in enumerate(phases(2, sample_of(k))):
            odd[slot_of(k), phase] = value

    def receive(k):
        local(k).wait()
        for copy in f_copies(k):
            copy.wait_recv()

    def step(k, _):
        @pl.when(k + AHEAD < CROSS)
        def _():
            for copy in z_copies(k + AHEAD):
                copy.start()

        @pl.when(k + 2 < CROSS)
        def _():
            start_y(k + 2)

        start_f(k + 1)
        receive(k)
        input_part(k)
        early_dot(k)

        @pl.when(k == HALO_AT)
        def _():
            @pl.when((slab > 0) & (slab != 8))
            def _():
                halo.wait_recv()

            @pl.when(slab == 8)
            def _():
                for q in range(4):
                    pltpu.make_async_remote_copy(
                        src_ref=planes.at[0, :, :, quarter(q)], dst_ref=planes.at[0, :, :, quarter(q)],
                        send_sem=h_send, recv_sem=halo_recv.at[q], device_id=mirror, device_id_type=MESH,
                    ).wait_recv()

            @pl.when(slab == 0)
            def _():
                planes[0] = jnp.zeros_like(planes[0])

            fill(late, LATE)

            def catch_up(n, _):
                late_dot(n)
                return 0

            lax.fori_loop(0, HALO_AT, catch_up, 0)

        @pl.when(k == 1)
        def _():
            cross_recv(0)
            cross_send(1)

        @pl.when(k == 3)
        def _():
            cross_recv(1)
            cross_send(2)

        @pl.when(k == 1)
        def _():
            @pl.when(low_side)
            def _():
                halo_out(0).wait_recv()
                halo_on.start()

        @pl.when(k >= HALO_AT)
        def _():
            late_dot(k)

        @pl.when(k >= 1)
        def _():
            pass_share(k - 1)
            finish(k - 1)

        return 0

    start_y(1)
    start_f(0)
    lax.fori_loop(0, CROSS - 1, step, 0)

    tail = CROSS - 1
    pair_copy = remote(acc.at[:, :, 1 - core], pair_in, c_send, c_recv, pair)

    def spread(d):
        to = (place + d + 1) % 8
        return remote(paired.at[to // 4, to % 4], near.at[d], r_send.at[d], r_recv.at[d], spread_to[d])

    cross_recv(2)
    early_dot(CROSS)
    late_dot(CROSS)
    input_part(CROSS)
    receive(tail)
    early_dot(tail)
    late_dot(tail)
    pair_copy.start()
    input_part(tail)
    pass_share(tail - 1)
    pair_copy.wait_recv()
    paired[...] = acc[:, :, core] + pair_in[...]
    for d in range(7):
        spread(d).start()
    pass_share(CROSS)
    finish(tail - 1)
    finish(CROSS)
    pass_share(tail)
    finish(tail)
    total = paired[half, column]
    for d in range(7):
        spread(d).wait_recv()
        total = total + near[d]
    scale = 1.0 / math.sqrt(2 * 16 * CELLS)
    wg_ref[...] = total * scale

    pair_copy.wait_send()
    for d in range(7):
        spread(d).wait_send()
    for copy in cross_y() + cross_f():
        copy.wait_send()
    for hop in range(3):
        cross_wait_send(hop)

    def drain(k, _):
        @pl.when(k < CROSS)
        def _():
            for copy in z_copies(k) + y_copies(k) + f_copies(k):
                copy.wait_send()

        @pl.when(slab > 0)
        def _():
            for q in range(4):
                share_copy(k, q).wait_send()

        @pl.when(high_side)
        def _():
            share_on(k).wait_send()

        return 0

    lax.fori_loop(0, CHUNKS, drain, 0)

    @pl.when((slab < 15) & (slab != 7))
    def _():
        halo.wait_send()

    @pl.when(slab == 7)
    def _():
        for q in range(4):
            halo_out(q).wait_send()

    @pl.when(low_side)
    def _():
        halo_on.wait_send()


def body(activations, out_grad, weights):
    planes = activations.transpose(2, 0, 1, 3)
    grad = out_grad.reshape(2, 16, CELLS)
    w = weights.reshape(216, 256)
    sem = pltpu.SemaphoreType.DMA
    f32, bf16 = jnp.float32, jnp.bfloat16
    any_space = pl.BlockSpec(memory_space=pl.ANY)
    vmem = pl.BlockSpec(memory_space=pltpu.VMEM)
    out, wg = pl.pallas_call(
        gather_kernel,
        out_shape=(
            jax.ShapeDtypeStruct((2, 2, 8, 4 * CELLS), bf16),
            jax.ShapeDtypeStruct((16, 256), f32),
        ),
        in_specs=[any_space, any_space, vmem],
        out_specs=(vmem, vmem),
        scratch_shapes=[
            pltpu.VMEM((CHUNKS, 4, 4, 16, CHUNK), bf16),
            pltpu.VMEM((CHUNKS, 128, CHUNK), bf16),
            pltpu.VMEM((CHUNKS, 96, CHUNK), bf16),
            pltpu.VMEM((3, 2, 8, 4 * CELLS), bf16),
            pltpu.VMEM((216, CHUNK), f32),
            pltpu.VMEM((2, 9, 8, 128), f32),
            pltpu.VMEM((CHUNKS, 4, 8, CHUNK), f32),
            pltpu.VMEM((CHUNKS, 4, 8, CHUNK), f32),
            pltpu.VMEM((3, 4, 8, CHUNK), f32),
            pltpu.VMEM((2, 4, 2, 16, 256), f32),
            pltpu.VMEM((2, 4, 16, 256), f32),
            pltpu.VMEM((2, 4, 16, 256), f32),
            pltpu.VMEM((7, 16, 256), f32),
            pltpu.VMEM((CHUNKS, 8, CHUNK), f32),
            pltpu.VMEM((2, 8, CELLS), bf16),
            sem((CHUNKS + 2,)),
            sem((CHUNKS, 3)), sem((CHUNKS, 3)),
            sem((CHUNKS, 2)), sem((CHUNKS, 2)),
            sem((CHUNKS, 3, 2)), sem((CHUNKS, 3, 2)),
            sem((CHUNKS, 2)), sem((CHUNKS, 2)),
            sem((4,)), sem((4,)),
            sem((CHUNKS, 4)), sem((CHUNKS, 4)),
            sem((CHUNKS,)), sem((CHUNKS,)),
            sem, sem,
            sem, sem,
            sem((7,)), sem((7,)),
            sem((2,)), sem((2,)),
            sem((2, 3)), sem((2, 3)),
        ],
        compiler_params=pltpu.CompilerParams(
            collective_id=0, has_side_effects=True, vmem_limit_bytes=48 * 1024 * 1024
        ),
    )(grad, planes, w)
    input_grad = out.transpose(1, 2, 0, 3)
    taps = wg[:, :216].reshape(16, 27, 8)
    taps = jnp.concatenate([taps[:, 18:], taps[:, :18]], axis=1)
    return input_grad, taps.transpose(1, 2, 0)


def solution(mesh):
    placed = (P(None, "chan", "slab", None), P(None, "chan", "slab", None), P(None, "chan", None))
    return jax.shard_map(
        body,
        mesh=mesh,
        in_specs=placed,
        out_specs=(P(None, "chan", "slab", None), P(None, "chan", "slab")),
        check_vma=False,
    )
```

```python
import functools
import math

import jax
import jax.numpy as jnp
from jax import lax
from jax.experimental import pallas as pl
from jax.experimental.pallas import tpu as pltpu
from jax.sharding import PartitionSpec as P

MESH = pl.DeviceIdType.MESH
EDGE = 128
HALF = EDGE // 2
CELLS = HALF * HALF
CHUNK = 1024
PER_SAMPLE = CELLS // CHUNK
CHUNKS = 2 * PER_SAMPLE
EARLY = tuple(range(9, 25))
HALO_AT = 4
AHEAD = 4
CROSS = CHUNKS - 1
LATE = (25, 26) + tuple(range(9))


def gather_kernel(
    grad_hbm, planes_hbm, w_ref, out_ref, wg_ref,
    held, early, late, planes, groups, carry, share, share_in,
    even, odd, mixed, acc, pair_in, paired, near, relay, halo_relay,
    local_sem, z_send, z_recv, o_send, o_recv, y_send, y_recv, f_send, f_recv,
    halo_send, halo_recv, p_send, p_recv, q_send, q_recv, h_send, h_recv,
    c_send, c_recv, r_send, r_recv, bf_send, bf_recv, bz_send, bz_recv,
):
    slab = lax.axis_index("slab")
    chan = lax.axis_index("chan")
    y, z = chan // 4, chan % 4
    half, spot = slab // 8, slab % 8

    def at(slab_to, chan_to):
        return (slab_to, chan_to)

    along_z = [at(slab, y * 4 + (z + d) % 4) for d in range(1, 4)]
    y_up = at(slab, ((y + 1) % 4) * 4 + z)
    y_down = at(slab, ((y + 3) % 4) * 4 + z)
    column, core = spot // 2, spot % 2
    near_to = [at(half * 8 + (spot + d) % 8, chan) for d in range(1, 8)]
    pair = at(slab + 1 - 2 * core, chan)
    place = half * 4 + column

    def core_peer(d):
        to = (place + d) % 8
        return at((to // 4) * 8 + (to % 4) * 2 + core, chan)

    spread_to = [core_peer(d) for d in range(1, 8)]
    across = [at((1 - half) * 8 + (spot + 2 * d) % 8, chan) for d in range(4)]
    mirror = at((1 - half) * 8 + spot, chan)
    before = at(lax.max(slab - 1, 0), chan)
    after = at(lax.min(slab + 1, 15), chan)
    low_side = (slab < 6) & (core == 1)
    high_side = (slab > 8) & (core == 0)

    barrier = pltpu.get_barrier_semaphore()
    peers = along_z + [y_up, y_down] + near_to + across

    def greet(peer):
        pl.semaphore_signal(barrier, inc=1, device_id=peer, device_id_type=MESH)

    for peer in peers:
        greet(peer)

    @pl.when(slab == 7)
    def _():
        for q in range(4):
            greet(at(8 + 2 * q, chan))

    @pl.when(slab == 8)
    def _():
        for q in range(4):
            greet(at(1 + 2 * q, chan))

    @pl.when(low_side)
    def _():
        greet(at(8, chan))

    @pl.when(high_side)
    def _():
        greet(at(7, chan))

    def sample_of(k):
        return ((k + 1) // PER_SAMPLE) % 2

    def begin_of(k):
        later = min(k // 3, 1) if isinstance(k, int) else lax.min(k // 3, 1)
        return (PER_SAMPLE - 1 - k + 3 * later + k // CROSS) * CHUNK

    def slot_of(k):
        return k % 2 + k // CROSS

    def source(k):
        return grad_hbm.at[sample_of(k), :, pl.ds(pl.multiple_of(begin_of(k), CHUNK), CHUNK)]

    def local(k):
        return pltpu.make_async_copy(source(k), held.at[k, y, z], local_sem.at[k])

    def remote(src, dst, send, recv, to):
        return pltpu.make_async_remote_copy(
            src_ref=src, dst_ref=dst, send_sem=send, recv_sem=recv, device_id=to, device_id_type=MESH
        )

    def z_copies(k):
        return [
            remote(source(k), held.at[k, y, z], z_send.at[k, d], z_recv.at[k, d], along_z[d])
            for d in range(3)
        ]

    low, high = (y + 3) % 4, (y + 1) % 4

    def y_own(k):
        return [
            remote(source(k), held.at[k, y, z], o_send.at[k, 0], o_recv.at[k, 0], y_up),
            remote(source(k), held.at[k, y, z], o_send.at[k, 1], o_recv.at[k, 1], y_down),
        ]

    def y_piece(k, d):
        piece = held.at[k, y, (z + 3 - d) % 4]
        return [
            remote(piece, piece, y_send.at[k, d, 0], y_recv.at[k, d, 0], y_up),
            remote(piece, piece, y_send.at[k, d, 1], y_recv.at[k, d, 1], y_down),
        ]

    def y_copies(k):
        return y_own(k) + y_piece(k, 0) + y_piece(k, 1) + y_piece(k, 2)

    def f_copies(k):
        from_low, from_high = held.at[k, low, pl.ds(0, 2)], held.at[k, high, pl.ds(2, 2)]
        return [
            remote(from_low, from_low, f_send.at[k, 0], f_recv.at[k, 0], y_up),
            remote(from_high, from_high, f_send.at[k, 1], f_recv.at[k, 1], y_down),
        ]

    def cross_y():
        return y_own(CROSS)

    def cross_f():
        from_low = held.at[CROSS, low, z, :, pl.ds(0, CHUNK // 2)]
        from_high = held.at[CROSS, high, z, :, pl.ds(CHUNK // 2, CHUNK // 2)]
        return [
            remote(from_low, from_low, bf_send.at[0], bf_recv.at[0], y_up),
            remote(from_high, from_high, bf_send.at[1], bf_recv.at[1], y_down),
        ]

    z_up = at(slab, y * 4 + lax.min(z + 1, 3))
    z_down = at(slab, y * 4 + lax.max(z - 1, 0))

    def cross_up(hop):
        piece = held.at[CROSS, :, lax.max(z - hop, 0)]
        return remote(piece, piece, bz_send.at[0, hop], bz_recv.at[0, hop], z_up)

    def cross_down(hop):
        piece = held.at[CROSS, :, lax.min(z + hop, 3)]
        return remote(piece, piece, bz_send.at[1, hop], bz_recv.at[1, hop], z_down)

    def cross_send(hop):
        @pl.when((z < 3) & (z >= hop))
        def _():
            cross_up(hop).start()

        @pl.when((z > 0) & (z + hop <= 3))
        def _():
            cross_down(hop).start()

    def cross_wait_send(hop):
        @pl.when((z < 3) & (z >= hop))
        def _():
            cross_up(hop).wait_send()

        @pl.when((z > 0) & (z + hop <= 3))
        def _():
            cross_down(hop).wait_send()

    def cross_recv(hop):
        @pl.when(z > hop)
        def _():
            cross_up(hop).wait_recv()

        @pl.when(z + hop < 3)
        def _():
            cross_down(hop).wait_recv()

    halo = remote(planes_hbm.at[1], planes.at[0], halo_send.at[0], halo_recv.at[0], after)

    def quarter(q):
        return pl.ds(pl.multiple_of(q * CELLS, CELLS), CELLS)

    def halo_out(q):
        if q == 3:
            return remote(
                planes_hbm.at[1, :, :, quarter(3)], planes.at[0, :, :, quarter(3)],
                halo_send.at[3], halo_recv.at[3], at(8, chan),
            )
        return remote(
            planes_hbm.at[1, :, :, quarter(q)], halo_relay,
            halo_send.at[q], h_recv, at(1 + 2 * q, chan),
        )

    halo_on = remote(
        halo_relay, planes.at[0, :, :, quarter(column)], h_send, halo_recv.at[column], at(8, chan)
    )
    load_even = pltpu.make_async_copy(planes_hbm.at[0], planes.at[1], local_sem.at[CHUNKS])
    load_odd = pltpu.make_async_copy(planes_hbm.at[1], planes.at[2], local_sem.at[CHUNKS + 1])

    def share_copy(k, q):
        return remote(share.at[k, q], share_in.at[k, q], p_send.at[k, q], p_recv.at[k, q], before)

    def share_out(k, q):
        if q == 0:
            return share_copy(k, 0)
        return remote(share.at[k, q], relay.at[k], p_send.at[k, q], q_recv.at[k], at(8 + 2 * q, chan))

    def share_on(k):
        return remote(relay.at[k], share_in.at[k, column], q_send.at[k], p_recv.at[k, column], at(7, chan))

    def send_share(k):
        @pl.when((slab > 0) & (slab != 8))
        def _():
            for q in range(4):
                share_copy(k, q).start()

        @pl.when(slab == 8)
        def _():
            for q in (1, 2, 3, 0):
                share_out(k, q).start()

    def pass_share(k):
        @pl.when(high_side)
        def _():
            share_out(k, 1).wait_recv()
            share_on(k).start()

    load_even.start()
    load_odd.start()
    for k in range(CHUNKS):
        local(k).start()

    is_edge = (slab == 7) | (slab == 8)
    is_side = low_side | high_side

    @pl.when(is_edge)
    def _():
        pl.semaphore_wait(barrier, len(peers) + 4)

    @pl.when(is_side)
    def _():
        pl.semaphore_wait(barrier, len(peers) + 1)

    @pl.when(jnp.logical_not(is_edge | is_side))
    def _():
        pl.semaphore_wait(barrier, len(peers))

    for copy in z_copies(0) + cross_y():
        copy.start()
    for k in range(CROSS):
        for copy in y_own(k) + (z_copies(k) if 0 < k < AHEAD else []):
            copy.start()

    @pl.when((slab < 15) & (slab != 7))
    def _():
        halo.start()

    @pl.when(slab == 7)
    def _():
        for q in range(4):
            halo_out(q).start()

    acc[...] = jnp.zeros_like(acc)
    carry[...] = jnp.zeros_like(carry)
    load_even.wait()
    load_odd.wait()

    lane = lax.broadcasted_iota(jnp.int32, (8, CELLS), 1)
    first_col = lane % HALF == 0
    first_row = lane < HALF

    def view(depth_tap, sample, row_tap, col_tap):
        at_block = (2 * (row_tap != 1) + (col_tap != 1)) * CELLS
        v = planes[depth_tap, sample, :, at_block : at_block + CELLS].astype(jnp.float32)
        amount = (HALF if row_tap == 0 else 0) + (1 if col_tap == 0 else 0)
        if amount:
            v = pltpu.roll(v, amount, 1)
            drop = first_col if col_tap == 0 else first_row
            if col_tap == 0 and row_tap == 0:
                drop = first_col | first_row
            v = jnp.where(drop, 0.0, v)
        return v

    def fill(store, taps):
        for sample in range(2):
            for pair in range((len(taps) + 1) // 2):
                rows = []
                for t in taps[2 * pair : 2 * pair + 2]:
                    rows.append(view(t // 9, sample, (t // 3) % 3, t % 3))
                if len(rows) == 1:
                    rows.append(jnp.zeros_like(rows[0]))
                both = jnp.concatenate(rows, axis=0).astype(jnp.bfloat16)
                for j in range(PER_SAMPLE):
                    k = 6 - j if sample else (CROSS if j == 0 else 3 - j)
                    store[k, 16 * pair : 16 * pair + 16, :] = both[
                        :, j * CHUNK : (j + 1) * CHUNK
                    ]

    def start_y(k):
        for d, copy in enumerate(z_copies(k)):
            copy.wait_recv()
            for onward in y_piece(k, d):
                onward.start()

    def start_f(k):
        for copy in y_copies(k):
            copy.wait_recv()
        for copy in f_copies(k):
            copy.start()

    for copy in cross_y():
        copy.wait_recv()
    for copy in cross_f():
        copy.start()
    start_y(0)
    fill(early, EARLY)
    local(CROSS).wait()
    for copy in cross_f():
        copy.wait_recv()
    cross_send(0)

    chunk_lane = lax.broadcasted_iota(jnp.int32, (8, CHUNK), 1)
    last_col = chunk_lane % HALF == HALF - 1

    def row_ahead(value, tail):
        wide = jnp.concatenate([value, tail], axis=1)
        return pltpu.roll(wide, CHUNK + 128 - HALF, 1)[:, :CHUNK]

    def col_ahead(value):
        return jnp.where(last_col, 0.0, pltpu.roll(value, CHUNK - 1, 1))

    def phases(depth_tap, sample):
        def fetch(row_tap, col_tap):
            row = 8 * (9 * depth_tap + 3 * row_tap + col_tap)
            return groups[row : row + 8, :]

        def odd_row(col_tap):
            at_carry = sample, 3 * depth_tap + col_tap
            moving = fetch(0, col_tap)
            moved = row_ahead(moving, carry[at_carry])
            carry[at_carry] = moving[:, :128]
            return fetch(2, col_tap) + moved

        found = []
        rows_even = [fetch(1, c) for c in range(3)]
        rows_odd = [odd_row(c) for c in range(3)]
        for rows in (rows_even, rows_odd):
            found.append(rows[1])
            found.append(rows[2] + col_ahead(rows[0]))
        return found

    def lanes_of(k, phase):
        return pl.ds(pl.multiple_of(phase * CELLS + begin_of(k), CHUNK), CHUNK)

    def late_dot(k):
        term = lax.dot_general(
            held[k].reshape(256, CHUNK), late[k], (((1,), (1,)), ((), ())), preferred_element_type=jnp.float32
        )
        acc[:, :, :, :, 128:224] += term.reshape(2, 4, 2, 16, 96)

    def finish(k):
        @pl.when(slab < 15)
        def _():
            for q in range(4):
                share_copy(k, q).wait_recv()

        for phase in range(4):
            value = odd[slot_of(k), phase]
            inward = jnp.where(slab < 15, share_in[k, phase], 0.0)
            value = value + inward
            same = even[slot_of(k), phase]
            blocks = []
            for b in range(CHUNK // 128):
                cut = slice(b * 128, b * 128 + 128)
                mixed[phase, b, pl.ds(0, 8, 2), :] = same[:, cut]
                mixed[phase, b, pl.ds(1, 8, 2), :] = value[:, cut]
                blocks.append(mixed[phase, b])
            out_ref[sample_of(k), :, lanes_of(k, phase)] = jnp.concatenate(blocks, axis=1).astype(jnp.bfloat16)

    def early_dot(k):
        term = lax.dot_general(
            held[k].reshape(256, CHUNK), early[k], (((1,), (1,)), ((), ())), preferred_element_type=jnp.float32
        )
        acc[:, :, :, :, :128] += term.reshape(2, 4, 2, 16, 128)

    def input_part(k):
        groups[...] = jnp.dot(w_ref[...], held[k].reshape(256, CHUNK), preferred_element_type=jnp.float32)
        for phase, value in enumerate(phases(0, sample_of(k))):
            share[k, phase] = value
        send_share(k)
        for phase, value in enumerate(phases(1, sample_of(k))):
            even[slot_of(k), phase] = value
        for phase, value in enumerate(phases(2, sample_of(k))):
            odd[slot_of(k), phase] = value

    def receive(k):
        local(k).wait()
        for copy in f_copies(k):
            copy.wait_recv()

    def step(k, _):
        @pl.when(k + AHEAD < CROSS)
        def _():
            for copy in z_copies(k + AHEAD):
                copy.start()

        @pl.when(k + 2 < CROSS)
        def _():
            start_y(k + 2)

        start_f(k + 1)
        receive(k)
        input_part(k)
        early_dot(k)

        @pl.when(k == HALO_AT)
        def _():
            @pl.when((slab > 0) & (slab != 8))
            def _():
                halo.wait_recv()

            @pl.when(slab == 8)
            def _():
                for q in range(4):
                    pltpu.make_async_remote_copy(
                        src_ref=planes.at[0, :, :, quarter(q)], dst_ref=planes.at[0, :, :, quarter(q)],
                        send_sem=h_send, recv_sem=halo_recv.at[q], device_id=mirror, device_id_type=MESH,
                    ).wait_recv()

            @pl.when(slab == 0)
            def _():
                planes[0] = jnp.zeros_like(planes[0])

            fill(late, LATE)

            def catch_up(n, _):
                late_dot(n)
                return 0

            lax.fori_loop(0, HALO_AT, catch_up, 0)

        @pl.when(k == 1)
        def _():
            cross_recv(0)
            cross_send(1)

        @pl.when(k == 3)
        def _():
            cross_recv(1)
            cross_send(2)

        @pl.when(k == 1)
        def _():
            @pl.when(low_side)
            def _():
                halo_out(0).wait_recv()
                halo_on.start()

        @pl.when(k >= HALO_AT)
        def _():
            late_dot(k)

        @pl.when(k >= 1)
        def _():
            pass_share(k - 1)
            finish(k - 1)

        return 0

    start_y(1)
    start_f(0)
    lax.fori_loop(0, CROSS - 1, step, 0)

    tail = CROSS - 1
    pair_copy = remote(acc.at[:, :, 1 - core], pair_in, c_send, c_recv, pair)

    def spread(d):
        to = (place + d + 1) % 8
        return remote(paired.at[to // 4, to % 4], near.at[d], r_send.at[d], r_recv.at[d], spread_to[d])

    cross_recv(2)
    early_dot(CROSS)
    late_dot(CROSS)
    input_part(CROSS)
    receive(tail)
    early_dot(tail)
    late_dot(tail)
    pair_copy.start()
    input_part(tail)
    pass_share(tail - 1)
    pair_copy.wait_recv()
    paired[...] = acc[:, :, core] + pair_in[...]
    for d in range(7):
        spread(d).start()
    pass_share(CROSS)
    finish(tail - 1)
    finish(CROSS)
    pass_share(tail)
    finish(tail)
    total = paired[half, column]
    for d in range(7):
        spread(d).wait_recv()
        total = total + near[d]
    scale = 1.0 / math.sqrt(2 * 16 * CELLS)
    wg_ref[...] = total * scale

    pair_copy.wait_send()
    for d in range(7):
        spread(d).wait_send()
    for copy in cross_y() + cross_f():
        copy.wait_send()
    for hop in range(3):
        cross_wait_send(hop)

    def drain(k, _):
        @pl.when(k < CROSS)
        def _():
            for copy in z_copies(k) + y_copies(k) + f_copies(k):
                copy.wait_send()

        @pl.when(slab > 0)
        def _():
            for q in range(4):
                share_copy(k, q).wait_send()

        @pl.when(high_side)
        def _():
            share_on(k).wait_send()

        return 0

    lax.fori_loop(0, CHUNKS, drain, 0)

    @pl.when((slab < 15) & (slab != 7))
    def _():
        halo.wait_send()

    @pl.when(slab == 7)
    def _():
        for q in range(4):
            halo_out(q).wait_send()

    @pl.when(low_side)
    def _():
        halo_on.wait_send()


def body(activations, out_grad, weights):
    planes = activations.transpose(2, 0, 1, 3)
    grad = out_grad.reshape(2, 16, CELLS)
    w = weights.reshape(216, 256)
    sem = pltpu.SemaphoreType.DMA
    f32, bf16 = jnp.float32, jnp.bfloat16
    any_space = pl.BlockSpec(memory_space=pl.ANY)
    vmem = pl.BlockSpec(memory_space=pltpu.VMEM)
    out, wg = pl.pallas_call(
        gather_kernel,
        out_shape=(
            jax.ShapeDtypeStruct((2, 16, 4 * CELLS), bf16),
            jax.ShapeDtypeStruct((16, 256), f32),
        ),
        in_specs=[any_space, any_space, vmem],
        out_specs=(vmem, vmem),
        scratch_shapes=[
            pltpu.VMEM((CHUNKS, 4, 4, 16, CHUNK), bf16),
            pltpu.VMEM((CHUNKS, 128, CHUNK), bf16),
            pltpu.VMEM((CHUNKS, 96, CHUNK), bf16),
            pltpu.VMEM((3, 2, 8, 4 * CELLS), bf16),
            pltpu.VMEM((216, CHUNK), f32),
            pltpu.VMEM((2, 9, 8, 128), f32),
            pltpu.VMEM((CHUNKS, 4, 8, CHUNK), f32),
            pltpu.VMEM((CHUNKS, 4, 8, CHUNK), f32),
            pltpu.VMEM((3, 4, 8, CHUNK), f32),
            pltpu.VMEM((3, 4, 8, CHUNK), f32),
            pltpu.VMEM((4, CHUNK // 128, 16, 128), f32),
            pltpu.VMEM((2, 4, 2, 16, 256), f32),
            pltpu.VMEM((2, 4, 16, 256), f32),
            pltpu.VMEM((2, 4, 16, 256), f32),
            pltpu.VMEM((7, 16, 256), f32),
            pltpu.VMEM((CHUNKS, 8, CHUNK), f32),
            pltpu.VMEM((2, 8, CELLS), bf16),
            sem((CHUNKS + 2,)),
            sem((CHUNKS, 3)), sem((CHUNKS, 3)),
            sem((CHUNKS, 2)), sem((CHUNKS, 2)),
            sem((CHUNKS, 3, 2)), sem((CHUNKS, 3, 2)),
            sem((CHUNKS, 2)), sem((CHUNKS, 2)),
            sem((4,)), sem((4,)),
            sem((CHUNKS, 4)), sem((CHUNKS, 4)),
            sem((CHUNKS,)), sem((CHUNKS,)),
            sem, sem,
            sem, sem,
            sem((7,)), sem((7,)),
            sem((2,)), sem((2,)),
            sem((2, 3)), sem((2, 3)),
        ],
        compiler_params=pltpu.CompilerParams(
            collective_id=0, has_side_effects=True, vmem_limit_bytes=48 * 1024 * 1024
        ),
    )(grad, planes, w)
    input_grad = out.reshape(2, 8, 2, 4 * CELLS)
    taps = wg[:, :216].reshape(16, 27, 8)
    taps = jnp.concatenate([taps[:, 18:], taps[:, :18]], axis=1)
    return input_grad, taps.transpose(1, 2, 0)


def solution(mesh):
    placed = (P(None, "chan", "slab", None), P(None, "chan", "slab", None), P(None, "chan", None))
    return jax.shard_map(
        body,
        mesh=mesh,
        in_specs=placed,
        out_specs=(P(None, "chan", "slab", None), P(None, "chan", "slab")),
        check_vma=False,
    )
```

```python
import functools
import math

import jax
import jax.numpy as jnp
from jax import lax
from jax.experimental import pallas as pl
from jax.experimental.pallas import tpu as pltpu
from jax.sharding import PartitionSpec as P

MESH = pl.DeviceIdType.MESH
EDGE = 128
HALF = EDGE // 2
CELLS = HALF * HALF
CHUNK = 1024
PER_SAMPLE = CELLS // CHUNK
CHUNKS = 2 * PER_SAMPLE
EARLY = tuple(range(9, 25))
HALO_AT = 4
AHEAD = 4
CROSS = CHUNKS - 1
LATE = (25, 26) + tuple(range(9))


def gather_kernel(
    grad_hbm, planes_hbm, w_ref, out_ref, wg_ref,
    held, early, late, planes, groups, carry, share, share_in,
    even, odd, mixed, acc, pair_in, paired, near, relay, halo_relay,
    local_sem, z_send, z_recv, o_send, o_recv, y_send, y_recv, f_send, f_recv,
    halo_send, halo_recv, p_send, p_recv, q_send, q_recv, h_send, h_recv,
    c_send, c_recv, r_send, r_recv, bf_send, bf_recv, bz_send, bz_recv,
):
    slab = lax.axis_index("slab")
    chan = lax.axis_index("chan")
    y, z = chan // 4, chan % 4
    half, spot = slab // 8, slab % 8

    def at(slab_to, chan_to):
        return (slab_to, chan_to)

    along_z = [at(slab, y * 4 + (z + d) % 4) for d in range(1, 4)]
    y_up = at(slab, ((y + 1) % 4) * 4 + z)
    y_down = at(slab, ((y + 3) % 4) * 4 + z)
    column, core = spot // 2, spot % 2
    near_to = [at(half * 8 + (spot + d) % 8, chan) for d in range(1, 8)]
    pair = at(slab + 1 - 2 * core, chan)
    place = half * 4 + column

    def core_peer(d):
        to = (place + d) % 8
        return at((to // 4) * 8 + (to % 4) * 2 + core, chan)

    spread_to = [core_peer(d) for d in range(1, 8)]
    across = [at((1 - half) * 8 + (spot + 2 * d) % 8, chan) for d in range(4)]
    mirror = at((1 - half) * 8 + spot, chan)
    before = at(lax.max(slab - 1, 0), chan)
    after = at(lax.min(slab + 1, 15), chan)
    low_side = (slab < 6) & (core == 1)
    high_side = (slab > 8) & (core == 0)

    barrier = pltpu.get_barrier_semaphore()
    peers = along_z + [y_up, y_down] + near_to + across

    def greet(peer):
        pl.semaphore_signal(barrier, inc=1, device_id=peer, device_id_type=MESH)

    for peer in peers:
        greet(peer)

    @pl.when(slab == 7)
    def _():
        for q in range(4):
            greet(at(8 + 2 * q, chan))

    @pl.when(slab == 8)
    def _():
        for q in range(4):
            greet(at(1 + 2 * q, chan))

    @pl.when(low_side)
    def _():
        greet(at(8, chan))

    @pl.when(high_side)
    def _():
        greet(at(7, chan))

    def sample_of(k):
        return ((k + 1) // PER_SAMPLE) % 2

    def begin_of(k):
        later = min(k // 3, 1) if isinstance(k, int) else lax.min(k // 3, 1)
        return (PER_SAMPLE - 1 - k + 3 * later + k // CROSS) * CHUNK

    def slot_of(k):
        return k % 3 + 2 * (k // CROSS)

    def source(k):
        return grad_hbm.at[sample_of(k), :, pl.ds(pl.multiple_of(begin_of(k), CHUNK), CHUNK)]

    def local(k):
        return pltpu.make_async_copy(source(k), held.at[k, y, z], local_sem.at[k])

    def remote(src, dst, send, recv, to):
        return pltpu.make_async_remote_copy(
            src_ref=src, dst_ref=dst, send_sem=send, recv_sem=recv, device_id=to, device_id_type=MESH
        )

    def z_copies(k):
        return [
            remote(source(k), held.at[k, y, z], z_send.at[k, d], z_recv.at[k, d], along_z[d])
            for d in range(3)
        ]

    low, high = (y + 3) % 4, (y + 1) % 4

    def y_own(k):
        return [
            remote(source(k), held.at[k, y, z], o_send.at[k, 0], o_recv.at[k, 0], y_up),
            remote(source(k), held.at[k, y, z], o_send.at[k, 1], o_recv.at[k, 1], y_down),
        ]

    def y_piece(k, d):
        piece = held.at[k, y, (z + 3 - d) % 4]
        return [
            remote(piece, piece, y_send.at[k, d, 0], y_recv.at[k, d, 0], y_up),
            remote(piece, piece, y_send.at[k, d, 1], y_recv.at[k, d, 1], y_down),
        ]

    def y_copies(k):
        return y_own(k) + y_piece(k, 0) + y_piece(k, 1) + y_piece(k, 2)

    def f_copies(k):
        from_low, from_high = held.at[k, low, pl.ds(0, 2)], held.at[k, high, pl.ds(2, 2)]
        return [
            remote(from_low, from_low, f_send.at[k, 0], f_recv.at[k, 0], y_up),
            remote(from_high, from_high, f_send.at[k, 1], f_recv.at[k, 1], y_down),
        ]

    def cross_y():
        return y_own(CROSS)

    def cross_f():
        from_low = held.at[CROSS, low, z, :, pl.ds(0, CHUNK // 2)]
        from_high = held.at[CROSS, high, z, :, pl.ds(CHUNK // 2, CHUNK // 2)]
        return [
            remote(from_low, from_low, bf_send.at[0], bf_recv.at[0], y_up),
            remote(from_high, from_high, bf_send.at[1], bf_recv.at[1], y_down),
        ]

    z_up = at(slab, y * 4 + lax.min(z + 1, 3))
    z_down = at(slab, y * 4 + lax.max(z - 1, 0))

    def cross_up(hop):
        piece = held.at[CROSS, :, lax.max(z - hop, 0)]
        return remote(piece, piece, bz_send.at[0, hop], bz_recv.at[0, hop], z_up)

    def cross_down(hop):
        piece = held.at[CROSS, :, lax.min(z + hop, 3)]
        return remote(piece, piece, bz_send.at[1, hop], bz_recv.at[1, hop], z_down)

    def cross_send(hop):
        @pl.when((z < 3) & (z >= hop))
        def _():
            cross_up(hop).start()

        @pl.when((z > 0) & (z + hop <= 3))
        def _():
            cross_down(hop).start()

    def cross_wait_send(hop):
        @pl.when((z < 3) & (z >= hop))
        def _():
            cross_up(hop).wait_send()

        @pl.when((z > 0) & (z + hop <= 3))
        def _():
            cross_down(hop).wait_send()

    def cross_recv(hop):
        @pl.when(z > hop)
        def _():
            cross_up(hop).wait_recv()

        @pl.when(z + hop < 3)
        def _():
            cross_down(hop).wait_recv()

    halo = remote(planes_hbm.at[1], planes.at[0], halo_send.at[0], halo_recv.at[0], after)

    def quarter(q):
        return pl.ds(pl.multiple_of(q * CELLS, CELLS), CELLS)

    def halo_out(q):
        if q == 3:
            return remote(
                planes_hbm.at[1, :, :, quarter(3)], planes.at[0, :, :, quarter(3)],
                halo_send.at[3], halo_recv.at[3], at(8, chan),
            )
        return remote(
            planes_hbm.at[1, :, :, quarter(q)], halo_relay,
            halo_send.at[q], h_recv, at(1 + 2 * q, chan),
        )

    halo_on = remote(
        halo_relay, planes.at[0, :, :, quarter(column)], h_send, halo_recv.at[column], at(8, chan)
    )
    load_even = pltpu.make_async_copy(planes_hbm.at[0], planes.at[1], local_sem.at[CHUNKS])
    load_odd = pltpu.make_async_copy(planes_hbm.at[1], planes.at[2], local_sem.at[CHUNKS + 1])

    def share_copy(k, q):
        return remote(share.at[k, q], share_in.at[k, q], p_send.at[k, q], p_recv.at[k, q], before)

    def share_out(k, q):
        if q == 0:
            return share_copy(k, 0)
        return remote(share.at[k, q], relay.at[k], p_send.at[k, q], q_recv.at[k], at(8 + 2 * q, chan))

    def share_on(k):
        return remote(relay.at[k], share_in.at[k, column], q_send.at[k], p_recv.at[k, column], at(7, chan))

    def send_share(k):
        @pl.when((slab > 0) & (slab != 8))
        def _():
            for q in range(4):
                share_copy(k, q).start()

        @pl.when(slab == 8)
        def _():
            for q in (1, 2, 3, 0):
                share_out(k, q).start()

    def pass_share(k):
        @pl.when(high_side)
        def _():
            share_out(k, 1).wait_recv()
            share_on(k).start()

    load_even.start()
    load_odd.start()
    for k in range(CHUNKS):
        local(k).start()

    is_edge = (slab == 7) | (slab == 8)
    is_side = low_side | high_side

    @pl.when(is_edge)
    def _():
        pl.semaphore_wait(barrier, len(peers) + 4)

    @pl.when(is_side)
    def _():
        pl.semaphore_wait(barrier, len(peers) + 1)

    @pl.when(jnp.logical_not(is_edge | is_side))
    def _():
        pl.semaphore_wait(barrier, len(peers))

    for copy in z_copies(0) + cross_y():
        copy.start()
    for k in range(CROSS):
        for copy in y_own(k) + (z_copies(k) if 0 < k < AHEAD else []):
            copy.start()

    @pl.when((slab < 15) & (slab != 7))
    def _():
        halo.start()

    @pl.when(slab == 7)
    def _():
        for q in range(4):
            halo_out(q).start()

    acc[...] = jnp.zeros_like(acc)
    carry[...] = jnp.zeros_like(carry)
    load_even.wait()
    load_odd.wait()

    lane = lax.broadcasted_iota(jnp.int32, (8, CELLS), 1)
    first_col = lane % HALF == 0
    first_row = lane < HALF

    def view(depth_tap, sample, row_tap, col_tap):
        at_block = (2 * (row_tap != 1) + (col_tap != 1)) * CELLS
        v = planes[depth_tap, sample, :, at_block : at_block + CELLS].astype(jnp.float32)
        amount = (HALF if row_tap == 0 else 0) + (1 if col_tap == 0 else 0)
        if amount:
            v = pltpu.roll(v, amount, 1)
            drop = first_col if col_tap == 0 else first_row
            if col_tap == 0 and row_tap == 0:
                drop = first_col | first_row
            v = jnp.where(drop, 0.0, v)
        return v

    def fill(store, taps):
        for sample in range(2):
            for pair in range((len(taps) + 1) // 2):
                rows = []
                for t in taps[2 * pair : 2 * pair + 2]:
                    rows.append(view(t // 9, sample, (t // 3) % 3, t % 3))
                if len(rows) == 1:
                    rows.append(jnp.zeros_like(rows[0]))
                both = jnp.concatenate(rows, axis=0).astype(jnp.bfloat16)
                for j in range(PER_SAMPLE):
                    k = 6 - j if sample else (CROSS if j == 0 else 3 - j)
                    store[k, 16 * pair : 16 * pair + 16, :] = both[
                        :, j * CHUNK : (j + 1) * CHUNK
                    ]

    def start_y(k):
        for d, copy in enumerate(z_copies(k)):
            copy.wait_recv()
            for onward in y_piece(k, d):
                onward.start()

    def start_f(k):
        for copy in y_copies(k):
            copy.wait_recv()
        for copy in f_copies(k):
            copy.start()

    for copy in cross_y():
        copy.wait_recv()
    for copy in cross_f():
        copy.start()
    start_y(0)
    fill(early, EARLY)
    local(CROSS).wait()
    for copy in cross_f():
        copy.wait_recv()
    cross_send(0)

    chunk_lane = lax.broadcasted_iota(jnp.int32, (8, CHUNK), 1)
    last_col = chunk_lane % HALF == HALF - 1

    def row_ahead(value, tail):
        wide = jnp.concatenate([value, tail], axis=1)
        return pltpu.roll(wide, CHUNK + 128 - HALF, 1)[:, :CHUNK]

    def col_ahead(value):
        return jnp.where(last_col, 0.0, pltpu.roll(value, CHUNK - 1, 1))

    def phases(depth_tap, sample):
        def fetch(row_tap, col_tap):
            row = 8 * (9 * depth_tap + 3 * row_tap + col_tap)
            return groups[row : row + 8, :]

        def odd_row(col_tap):
            at_carry = sample, 3 * depth_tap + col_tap
            moving = fetch(0, col_tap)
            moved = row_ahead(moving, carry[at_carry])
            carry[at_carry] = moving[:, :128]
            return fetch(2, col_tap) + moved

        found = []
        rows_even = [fetch(1, c) for c in range(3)]
        rows_odd = [odd_row(c) for c in range(3)]
        for rows in (rows_even, rows_odd):
            found.append(rows[1])
            found.append(rows[2] + col_ahead(rows[0]))
        return found

    def lanes_of(k, phase):
        return pl.ds(pl.multiple_of(phase * CELLS + begin_of(k), CHUNK), CHUNK)

    def late_dot(k):
        term = lax.dot_general(
            held[k].reshape(256, CHUNK), late[k], (((1,), (1,)), ((), ())), preferred_element_type=jnp.float32
        )
        acc[:, :, :, :, 128:224] += term.reshape(2, 4, 2, 16, 96)

    def finish(k):
        @pl.when(slab < 15)
        def _():
            for q in range(4):
                share_copy(k, q).wait_recv()

        for phase in range(4):
            value = odd[slot_of(k), phase]
            inward = jnp.where(slab < 15, share_in[k, phase], 0.0)
            value = value + inward
            same = even[slot_of(k), phase]
            blocks = []
            for b in range(CHUNK // 128):
                cut = slice(b * 128, b * 128 + 128)
                mixed[phase, b, pl.ds(0, 8, 2), :] = same[:, cut]
                mixed[phase, b, pl.ds(1, 8, 2), :] = value[:, cut]
                blocks.append(mixed[phase, b])
            out_ref[sample_of(k), :, lanes_of(k, phase)] = jnp.concatenate(blocks, axis=1).astype(jnp.bfloat16)

    def early_dot(k):
        term = lax.dot_general(
            held[k].reshape(256, CHUNK), early[k], (((1,), (1,)), ((), ())), preferred_element_type=jnp.float32
        )
        acc[:, :, :, :, :128] += term.reshape(2, 4, 2, 16, 128)

    def input_part(k):
        groups[...] = jnp.dot(w_ref[...], held[k].reshape(256, CHUNK), preferred_element_type=jnp.float32)
        for phase, value in enumerate(phases(0, sample_of(k))):
            share[k, phase] = value
        send_share(k)
        for phase, value in enumerate(phases(1, sample_of(k))):
            even[slot_of(k), phase] = value
        for phase, value in enumerate(phases(2, sample_of(k))):
            odd[slot_of(k), phase] = value

    def receive(k):
        local(k).wait()
        for copy in f_copies(k):
            copy.wait_recv()

    def step(k, _):
        @pl.when(k + AHEAD < CROSS)
        def _():
            for copy in z_copies(k + AHEAD):
                copy.start()

        @pl.when(k + 2 < CROSS)
        def _():
            start_y(k + 2)

        start_f(k + 1)
        receive(k)
        input_part(k)
        early_dot(k)

        @pl.when(k == HALO_AT)
        def _():
            @pl.when((slab > 0) & (slab != 8))
            def _():
                halo.wait_recv()

            @pl.when(slab == 8)
            def _():
                for q in range(4):
                    pltpu.make_async_remote_copy(
                        src_ref=planes.at[0, :, :, quarter(q)], dst_ref=planes.at[0, :, :, quarter(q)],
                        send_sem=h_send, recv_sem=halo_recv.at[q], device_id=mirror, device_id_type=MESH,
                    ).wait_recv()

            @pl.when(slab == 0)
            def _():
                planes[0] = jnp.zeros_like(planes[0])

            fill(late, LATE)

            def catch_up(n, _):
                late_dot(n)
                return 0

            lax.fori_loop(0, HALO_AT, catch_up, 0)

        @pl.when(k == 1)
        def _():
            cross_recv(0)
            cross_send(1)

        @pl.when(k == 3)
        def _():
            cross_recv(1)
            cross_send(2)

        @pl.when(k == 1)
        def _():
            @pl.when(low_side)
            def _():
                halo_out(0).wait_recv()
                halo_on.start()

        @pl.when(k >= HALO_AT)
        def _():
            late_dot(k)

        @pl.when(k >= 1)
        def _():
            pass_share(k - 1)

        @pl.when(k >= 2)
        def _():
            finish(k - 2)

        return 0

    start_y(1)
    start_f(0)
    lax.fori_loop(0, CROSS - 1, step, 0)

    tail = CROSS - 1
    pair_copy = remote(acc.at[:, :, 1 - core], pair_in, c_send, c_recv, pair)

    def spread(d):
        to = (place + d + 1) % 8
        return remote(paired.at[to // 4, to % 4], near.at[d], r_send.at[d], r_recv.at[d], spread_to[d])

    cross_recv(2)
    early_dot(CROSS)
    late_dot(CROSS)
    input_part(CROSS)
    receive(tail)
    early_dot(tail)
    late_dot(tail)
    pair_copy.start()
    input_part(tail)
    pass_share(tail - 1)
    pair_copy.wait_recv()
    paired[...] = acc[:, :, core] + pair_in[...]
    for d in range(7):
        spread(d).start()
    pass_share(CROSS)
    finish(tail - 2)
    finish(tail - 1)
    finish(CROSS)
    pass_share(tail)
    finish(tail)
    total = paired[half, column]
    for d in range(7):
        spread(d).wait_recv()
        total = total + near[d]
    scale = 1.0 / math.sqrt(2 * 16 * CELLS)
    wg_ref[...] = total * scale

    pair_copy.wait_send()
    for d in range(7):
        spread(d).wait_send()
    for copy in cross_y() + cross_f():
        copy.wait_send()
    for hop in range(3):
        cross_wait_send(hop)

    def drain(k, _):
        @pl.when(k < CROSS)
        def _():
            for copy in z_copies(k) + y_copies(k) + f_copies(k):
                copy.wait_send()

        @pl.when(slab > 0)
        def _():
            for q in range(4):
                share_copy(k, q).wait_send()

        @pl.when(high_side)
        def _():
            share_on(k).wait_send()

        return 0

    lax.fori_loop(0, CHUNKS, drain, 0)

    @pl.when((slab < 15) & (slab != 7))
    def _():
        halo.wait_send()

    @pl.when(slab == 7)
    def _():
        for q in range(4):
            halo_out(q).wait_send()

    @pl.when(low_side)
    def _():
        halo_on.wait_send()


def body(activations, out_grad, weights):
    planes = activations.transpose(2, 0, 1, 3)
    grad = out_grad.reshape(2, 16, CELLS)
    w = weights.reshape(216, 256)
    sem = pltpu.SemaphoreType.DMA
    f32, bf16 = jnp.float32, jnp.bfloat16
    any_space = pl.BlockSpec(memory_space=pl.ANY)
    vmem = pl.BlockSpec(memory_space=pltpu.VMEM)
    out, wg = pl.pallas_call(
        gather_kernel,
        out_shape=(
            jax.ShapeDtypeStruct((2, 16, 4 * CELLS), bf16),
            jax.ShapeDtypeStruct((16, 256), f32),
        ),
        in_specs=[any_space, any_space, vmem],
        out_specs=(vmem, vmem),
        scratch_shapes=[
            pltpu.VMEM((CHUNKS, 4, 4, 16, CHUNK), bf16),
            pltpu.VMEM((CHUNKS, 128, CHUNK), bf16),
            pltpu.VMEM((CHUNKS, 96, CHUNK), bf16),
            pltpu.VMEM((3, 2, 8, 4 * CELLS), bf16),
            pltpu.VMEM((216, CHUNK), f32),
            pltpu.VMEM((2, 9, 8, 128), f32),
            pltpu.VMEM((CHUNKS, 4, 8, CHUNK), f32),
            pltpu.VMEM((CHUNKS, 4, 8, CHUNK), f32),
            pltpu.VMEM((4, 4, 8, CHUNK), f32),
            pltpu.VMEM((4, 4, 8, CHUNK), f32),
            pltpu.VMEM((4, CHUNK // 128, 16, 128), f32),
            pltpu.VMEM((2, 4, 2, 16, 256), f32),
            pltpu.VMEM((2, 4, 16, 256), f32),
            pltpu.VMEM((2, 4, 16, 256), f32),
            pltpu.VMEM((7, 16, 256), f32),
            pltpu.VMEM((CHUNKS, 8, CHUNK), f32),
            pltpu.VMEM((2, 8, CELLS), bf16),
            sem((CHUNKS + 2,)),
            sem((CHUNKS, 3)), sem((CHUNKS, 3)),
            sem((CHUNKS, 2)), sem((CHUNKS, 2)),
            sem((CHUNKS, 3, 2)), sem((CHUNKS, 3, 2)),
            sem((CHUNKS, 2)), sem((CHUNKS, 2)),
            sem((4,)), sem((4,)),
            sem((CHUNKS, 4)), sem((CHUNKS, 4)),
            sem((CHUNKS,)), sem((CHUNKS,)),
            sem, sem,
            sem, sem,
            sem((7,)), sem((7,)),
            sem((2,)), sem((2,)),
            sem((2, 3)), sem((2, 3)),
        ],
        compiler_params=pltpu.CompilerParams(
            collective_id=0, has_side_effects=True, vmem_limit_bytes=48 * 1024 * 1024
        ),
    )(grad, planes, w)
    input_grad = out.reshape(2, 8, 2, 4 * CELLS)
    taps = wg[:, :216].reshape(16, 27, 8)
    taps = jnp.concatenate([taps[:, 18:], taps[:, :18]], axis=1)
    return input_grad, taps.transpose(1, 2, 0)


def solution(mesh):
    placed = (P(None, "chan", "slab", None), P(None, "chan", "slab", None), P(None, "chan", None))
    return jax.shard_map(
        body,
        mesh=mesh,
        in_specs=placed,
        out_specs=(P(None, "chan", "slab", None), P(None, "chan", "slab")),
        check_vma=False,
    )
```
